128 devices in a mesh: gx: 8 (over x_hi, y), gy: 4 (over x_lo, core), gz: 4 (over z).
Axes of the slice: x: 4 (x_hi: 2, x_lo: 2; x = x_hi * 2 + x_lo), y: 4, z: 4, core: 2. Of those that a mesh axis runs over, the one named last changes fastest.
Arguments:
- preact: bfloat16 [16384, 12288], P('gx', 'gy'), may hold values from -6 to 6
- grad_output: bfloat16 [16384, 4608], P(('gx', 'gy'), 'gz'), may hold values from -1.5 to 1.5
- down_weight: bfloat16 [12288, 4608], P('gy', 'gz'), may hold values from -0.09375 to 0.09375
Outputs:
- grad_pre: bfloat16 [16384, 12288], P(('gx', 'gz'), 'gy')
- grad_down: bfloat16 [12288, 4608], P(('gy', 'gx'), 'gz')
The draws below stay inside these ranges and needn't reach their ends.
All inputs are finite; a program needn't handle non-finite values.
Results may differ from the reference program's by a relative error of at most 0.013.
Values may be sent and summed in bfloat16 or wider, within the bound.
No kernel may reach another device: no remote copies, remote signals or barrier semaphores. Data moves between devices by JAX's collectives and lax.ppermute only.
A program may use at most 256 MiB of HBM per device.

```python
import math
import jax
import jax.numpy as jnp
from jax import lax

D = 4608
FF = 12288
ROW_BLOCK = 2048
ROWS = 16384
N_GX = 8
N_GZ = 4


def steps_of(stream_key, dims, split, smallest, top_value):
    loudness = 1.0
    for position, parts in split:
        heights = jax.random.uniform(jax.random.fold_in(jax.random.fold_in(stream_key, 6), position), (parts,), jnp.float32, smallest / len(split), top_value / len(split))
        loudness = loudness * jnp.repeat(jnp.exp(heights), dims[position] // parts).reshape((-1,) + (1,) * (len(dims) - 1 - position))
    return loudness


def centred(own_key, extent, scale, limit, shards=(), kind=jnp.bfloat16):
    drawn = scale * jax.random.normal(own_key, extent, jnp.float32)
    if shards:
        drawn = drawn * steps_of(own_key, extent, shards, -0.22, 0.18)
    return jnp.clip(drawn, -limit, limit).astype(kind)


def setup_inputs(seed: int = 0) -> dict:
    key_of = jax.random.split(jax.random.key(seed), 4)
    preact = centred(key_of[0], (ROWS, FF), 1.0, 6.0, ((0, 8), (1, 4)))
    grad_output = centred(key_of[1], (ROWS, D), 0.25, 1.5, ((0, 32), (1, 4)))
    down_weight = centred(key_of[2], (FF, D), D ** -0.5, 0.09375, ((0, 4), (1, 4)))
    return {"preact": preact, "grad_output": grad_output, "down_weight": down_weight}


root_half = 1.0 / math.sqrt(2.0)
slope_scale = 1.0 / math.sqrt(2.0 * math.pi)

def gaussian_unit(values):
    return 0.5 * values * (1.0 + lax.erf(values * root_half))

def unit_slope(values):
    return 0.5 * (1.0 + lax.erf(values * root_half)) + values * jnp.exp(-0.5 * values * values) * slope_scale

def reference(preact, grad_output, down_weight):
    pre_wide = preact.astype(jnp.float32)
    activation = gaussian_unit(pre_wide).astype(jnp.bfloat16)
    feature_block = D // N_GZ
    contract_cols = (((1,), (1,)), ((), ()))

    def add_part(carry, index):
        start = (index * feature_block).astype(jnp.int32)
        out_cols = lax.dynamic_slice_in_dim(grad_output, start, feature_block, 1)
        weight_cols = lax.dynamic_slice_in_dim(down_weight, start, feature_block, 1)
        part = lax.dot_general(out_cols, weight_cols, contract_cols, preferred_element_type=jnp.float32).astype(jnp.bfloat16)
        part = lax.optimization_barrier(part)
        return (carry + part.astype(jnp.float32), None)
    grad_act, unused = lax.scan(add_part, jnp.zeros((ROWS, FF), jnp.float32), jnp.arange(N_GZ, dtype=jnp.int32))
    grad_pre = (grad_act * unit_slope(pre_wide)).astype(jnp.bfloat16)
    blocks = (activation.reshape(N_GX, ROW_BLOCK, FF), grad_output.reshape(N_GX, ROW_BLOCK, D))

    def accumulate(carry, block):
        act_block, output_block = block
        down_term = jnp.dot(act_block.T, output_block, preferred_element_type=jnp.float32).astype(jnp.bfloat16)
        down_term = lax.optimization_barrier(down_term)
        return (carry + down_term.astype(jnp.float32), None)
    down_sum, unused2 = lax.scan(accumulate, jnp.zeros((FF, D), jnp.float32), blocks)
    return (grad_pre, down_sum.astype(jnp.bfloat16))
```

```python
import math

import jax
import jax.numpy as jnp
from jax import lax
from jax.sharding import PartitionSpec as P

root_half = 1.0 / math.sqrt(2.0)
slope_scale = 1.0 / math.sqrt(2.0 * math.pi)
STAGES = ((0, 128), (128, 256), (256, 384), (384, 512))
bf16 = jnp.bfloat16
f32 = jnp.float32


def unit_slope(values):
    return (
        0.5 * (1.0 + lax.erf(values * root_half))
        + values * jnp.exp(-0.5 * values * values) * slope_scale
    )


def gz_ring(step):
    return [(i, (i + step) % 4) for i in range(4)]


def gx_move(dh, dy):
    return [(h * 4 + y, (h + dh) % 2 * 4 + (y + dy) % 4) for h in range(2) for y in range(4)]


def gy_move(dl, dc):
    return [(l * 2 + c, (l + dl) % 2 * 2 + (c + dc) % 2) for l in range(2) for c in range(2)]


def after(value, *others):
    return lax.optimization_barrier((value,) + others)[0]


def shards(preact, grad_output, down_weight):
    gy = lax.axis_index("gy")
    gz = lax.axis_index("gz")
    gx = lax.axis_index("gx")
    core, lo = gy % 2, gy // 2
    y = gx % 4
    h = gx // 4

    contract_cols = (((1,), (1,)), ((), ()))
    contract_rows = (((0,), (0,)), ((), ()))

    gathered = []
    scattered = []
    previous = None
    for start, stop in STAGES:
        own = grad_output[start:stop]
        if previous is not None:
            own = after(own, previous)
        across = lax.ppermute(own, "gy", gy_move(1, 0))
        partner = lax.ppermute(own, "gy", gy_move(0, 1))
        corner = lax.ppermute(across, "gy", gy_move(0, 1))
        previous = across
        near = jnp.where(core == 0, jnp.stack((own, partner)), jnp.stack((partner, own)))
        far = jnp.where(core == 0, jnp.stack((across, corner)), jnp.stack((corner, across)))
        pieces = jnp.where(lo == 0, jnp.concatenate((near, far)), jnp.concatenate((far, near)))
        gathered.append(pieces)
    for pieces in gathered:
        rows = pieces.reshape(-1, pieces.shape[-1])
        part = lax.dot_general(rows, down_weight, contract_cols, preferred_element_type=f32)
        scattered.append(
            lax.psum_scatter(part.astype(bf16), "gz", scatter_dimension=0, tiled=True)
        )

    pre_wide = preact.astype(f32)
    activation = (0.5 * pre_wide * (1.0 + lax.erf(pre_wide * root_half))).astype(bf16)
    output_rows = jnp.concatenate(gathered, axis=1).reshape(-1, grad_output.shape[1])
    chunk = preact.shape[1] // 8

    def term(h_dest, y_dest):
        cols = lax.dynamic_slice_in_dim(activation, (h_dest * 4 + y_dest) * chunk, chunk, 1)
        return lax.dot_general(cols, output_rows, contract_rows, preferred_element_type=f32)

    up, down = gx_move(0, 1), gx_move(0, -1)
    y_up, y_down, y_far = (y + 1) % 4, (y + 3) % 4, (y + 2) % 4
    a_far = lax.ppermute(term(0, y_far).astype(bf16), "gx", down)
    b_far = lax.ppermute(term(1, y_far).astype(bf16), "gx", up)
    a_side = lax.ppermute(term(0, y_up).astype(bf16), "gx", up)
    b_side = lax.ppermute(term(1, y_down).astype(bf16), "gx", down)
    a_sum = lax.ppermute((term(0, y_down) + a_far.astype(f32)).astype(bf16), "gx", down)
    b_sum = lax.ppermute((term(1, y_up) + b_far.astype(f32)).astype(bf16), "gx", up)
    a_own = term(0, y) + a_side.astype(f32) + a_sum.astype(f32)
    b_own = term(1, y) + b_side.astype(f32) + b_sum.astype(f32)
    keep = jnp.where(h == 0, a_own, b_own)
    give = jnp.where(h == 0, b_own, a_own).astype(bf16)
    taken = lax.ppermute(give, "gx", gx_move(1, 0))
    grad_down = (keep + taken.astype(f32)).astype(bf16)

    outs = []
    for (start, stop), summed in zip(STAGES, scattered):
        rows = lax.dynamic_slice_in_dim(preact, gz * 512 + start, stop - start, 0).astype(f32)
        outs.append((summed.astype(f32) * unit_slope(rows)).astype(bf16))
    grad_pre = jnp.concatenate(outs)
    return (grad_pre, grad_down)


def solution(mesh):
    return jax.shard_map(
        shards,
        mesh=mesh,
        in_specs=(P("gx", "gy"), P(("gx", "gy"), "gz"), P("gy", "gz")),
        out_specs=(P(("gx", "gz"), "gy"), P(("gy", "gx"), "gz")),
        check_vma=False,
    )
```

```python
import functools
import math

import jax
import jax.numpy as jnp
from jax import lax
from jax.experimental import pallas as pl
from jax.experimental.pallas import tpu as pltpu
from jax.sharding import PartitionSpec as P

root_half = 1.0 / math.sqrt(2.0)
slope_scale = 1.0 / math.sqrt(2.0 * math.pi)
bf16 = jnp.bfloat16
f32 = jnp.float32
HEAD = 128
TILE = 512
COLS = 384
COST = 64
VMEM = 63 * 1024 * 1024


def gelu(values):
    return 0.5 * values * (1.0 + lax.erf(values * root_half))


def unit_slope(values):
    return (
        0.5 * (1.0 + lax.erf(values * root_half))
        + values * jnp.exp(-0.5 * values * values) * slope_scale
    )


def gz_ring(step):
    return [(i, (i + step) % 4) for i in range(4)]


def gx_move(dh, dy):
    return [(h * 4 + y, (h + dh) % 2 * 4 + (y + dy) % 4) for h in range(2) for y in range(4)]


def gy_move(dl, dc):
    return [(l * 2 + c, (l + dl) % 2 * 2 + (c + dc) % 2) for l in range(2) for c in range(2)]


def after(value, *others):
    return lax.optimization_barrier((value,) + others)[0]


def call(body, name, grid, prefetch, in_specs, out_specs, out_shape, flops, moved, **extra):
    return pl.pallas_call(
        body,
        name=name,
        out_shape=out_shape,
        grid_spec=pltpu.PrefetchScalarGridSpec(
            num_scalar_prefetch=prefetch, grid=grid, in_specs=in_specs, out_specs=out_specs
        ),
        compiler_params=pltpu.CompilerParams(
            dimension_semantics=("arbitrary",) * len(grid), vmem_limit_bytes=VMEM
        ),
        cost_estimate=pl.CostEstimate(
            flops=int(flops) // COST, bytes_accessed=int(moved) // COST, transcendentals=0
        ),
        **extra,
    )


def rows_dot(rows, weights):
    return lax.dot_general(rows, weights, (((1,), (1,)), ((), ())), preferred_element_type=f32)


def plain_dot(left, right):
    return lax.dot_general(left, right, (((1,), (0,)), ((), ())), preferred_element_type=f32)


ORDER, FAR, UP, DOWN, OWN, GZ, Y_FAR, Y_UP, Y_DOWN, Y, H = 0, 4, 5, 6, 7, 8, 9, 10, 11, 12, 13


def gelu_body(table, pre, head, tail):
    act = gelu(pre[...].astype(f32)).astype(bf16)
    head[...] = act[: head.shape[1]].T
    tail[...] = act[head.shape[1] :].T


def transposed_gelu(preact, table, half):
    rows, hidden = preact.shape
    piece = rows // 4
    tiles = hidden // 2 // TILE
    tail = piece - HEAD
    return call(
        gelu_body,
        "gelu_t",
        (tiles, 4),
        1,
        [pl.BlockSpec((piece, TILE), lambda t, j, o: (o[ORDER + j], half * tiles + t))],
        [
            pl.BlockSpec((TILE, HEAD), lambda t, j, o: (t, j)),
            pl.BlockSpec((TILE, tail), lambda t, j, o: (t, j)),
        ],
        [
            jax.ShapeDtypeStruct((hidden // 2, 4 * HEAD), bf16),
            jax.ShapeDtypeStruct((hidden // 2, 4 * tail), bf16),
        ],
        rows * hidden * 40,
        rows * hidden * 2,
    )(table, preact)


def tail_body(table, rows, weights, out):
    for r in range(4):
        out[r] = rows_dot(rows[table[ORDER + r]], weights[...]).astype(bf16)


def tail_parts(rows, weights, table):
    _, count, depth = rows.shape
    hidden = weights.shape[0]
    return call(
        tail_body,
        "tail_parts",
        (hidden // TILE,),
        1,
        [
            pl.BlockSpec((4, count, depth), lambda t, o: (0, 0, 0)),
            pl.BlockSpec((TILE, depth), lambda t, o: (t, 0)),
        ],
        pl.BlockSpec((4, count, TILE), lambda t, o: (0, 0, t)),
        jax.ShapeDtypeStruct((4, count, hidden), bf16),
        8 * count * depth * hidden,
        2 * (4 * count * depth + depth * hidden + 4 * count * hidden),
    )(table, rows, weights)


def head_body(adds, table, rows_a, rows_b, weights_a, weights_b, *refs):
    out_a, out_b = refs[-2:]
    sum_a = rows_dot(rows_a[0], weights_a[...])
    sum_b = rows_dot(rows_b[0], weights_b[...])
    if adds:
        sum_a += refs[0][...].astype(f32)
        sum_b += refs[1][...].astype(f32)
    out_a[...] = sum_a.astype(bf16)
    out_b[...] = sum_b.astype(bf16)


def head_parts(rows, weights, table, at_a, at_b, *arrived):
    _, count, depth = rows.shape
    hidden = weights.shape[0]
    tiles = hidden // 2 // TILE
    half = pl.BlockSpec((count, TILE), lambda t, p: (0, t))
    shape = jax.ShapeDtypeStruct((count, hidden // 2), bf16)
    return call(
        functools.partial(head_body, bool(arrived)),
        "head_parts",
        (tiles,),
        1,
        [
            pl.BlockSpec((1, count, depth), lambda t, p: (p[at_a], 0, 0)),
            pl.BlockSpec((1, count, depth), lambda t, p: (p[at_b], 0, 0)),
            pl.BlockSpec((TILE, depth), lambda t, p: (t, 0)),
            pl.BlockSpec((TILE, depth), lambda t, p: (tiles + t, 0)),
        ]
        + [half] * len(arrived),
        [half, half],
        [shape, shape],
        2 * count * depth * hidden,
        2 * (2 * count * depth + depth * hidden + count * hidden * (1 + len(arrived) // 2)),
    )(table, rows, rows, weights, weights, *arrived)


def head_last_body(table, rows, weights, pre, side_a, sum_a, side_b, sum_b, out):
    total = rows_dot(rows[0], weights[...])
    slope = unit_slope(pre[...].astype(f32))
    first = pl.program_id(0) < pl.num_programs(0) // 2

    @pl.when(first)
    def _():
        whole = total + side_a[...].astype(f32) + sum_a[...].astype(f32)
        out[...] = (whole * slope).astype(bf16)

    @pl.when(jnp.logical_not(first))
    def _():
        whole = total + side_b[...].astype(f32) + sum_b[...].astype(f32)
        out[...] = (whole * slope).astype(bf16)


def head_last(rows, weights, preact, table, side_a, sum_a, side_b, sum_b):
    share = preact.shape[0] // 4
    _, count, depth = rows.shape
    hidden = weights.shape[0]
    tiles = hidden // TILE
    half_a = pl.BlockSpec((count, TILE), lambda t, p: (0, jnp.minimum(t, tiles // 2 - 1)))
    half_b = pl.BlockSpec((count, TILE), lambda t, p: (0, jnp.maximum(t - tiles // 2, 0)))
    return call(
        head_last_body,
        "head_last",
        (tiles,),
        1,
        [
            pl.BlockSpec((1, count, depth), lambda t, p: (p[OWN], 0, 0)),
            pl.BlockSpec((TILE, depth), lambda t, p: (t, 0)),
            pl.BlockSpec((count, TILE), lambda t, p: (p[GZ] * (share // count), t)),
            half_a,
            half_a,
            half_b,
            half_b,
        ],
        pl.BlockSpec((count, TILE), lambda t, p: (0, t)),
        jax.ShapeDtypeStruct((share, hidden), bf16),
        2 * count * depth * hidden,
        2 * (count * depth + depth * hidden + 4 * count * hidden),
    )(table, rows, weights, preact, side_a, sum_a, side_b, sum_b)


def tail_last_body(table, summed, pre, held, out):
    out[...] = (summed[...].astype(f32) * unit_slope(pre[...].astype(f32))).astype(bf16)


def tail_last(summed, preact, table, held):
    count, hidden = summed.shape
    step = 128
    start = HEAD // step
    return call(
        tail_last_body,
        "tail_last",
        (count // step,),
        1,
        [
            pl.BlockSpec((step, hidden), lambda t, p: (t, 0)),
            pl.BlockSpec((step, hidden), lambda t, p: (p[GZ] * (held.shape[0] // step) + start + t, 0)),
            pl.BlockSpec(memory_space=pl.ANY),
        ],
        pl.BlockSpec((step, hidden), lambda t, p: (start + t, 0)),
        jax.ShapeDtypeStruct(held.shape, bf16),
        count * hidden * 40,
        6 * count * hidden,
        input_output_aliases={3: 0},
    )(table, summed, preact, held)


def term_of(left_head, left_tail, right_head, right_tail):
    return plain_dot(left_head[...], right_head[...]) + plain_dot(left_tail[...], right_tail[...])


def terms_body(adds, table, a_head, a_tail, b_head, b_tail, g_head, g_tail, *refs):
    out_a, out_b = refs[-2:]
    sum_a = term_of(a_head, a_tail, g_head, g_tail)
    sum_b = term_of(b_head, b_tail, g_head, g_tail)
    if adds:
        sum_a += refs[0][...].astype(f32)
        sum_b += refs[1][...].astype(f32)
    out_a[...] = sum_a.astype(bf16)
    out_b[...] = sum_b.astype(bf16)


def last_terms_body(table, a_head, a_tail, b_head, b_tail, g_head, g_tail, *refs):
    side_a, sum_a, side_b, sum_b, keep, give = refs
    whole_a = term_of(a_head, a_tail, g_head, g_tail)
    whole_a += side_a[...].astype(f32) + sum_a[...].astype(f32)
    whole_b = term_of(b_head, b_tail, g_head, g_tail)
    whole_b += side_b[...].astype(f32) + sum_b[...].astype(f32)
    first = table[H] == 0
    keep[...] = jnp.where(first, whole_a, whole_b)
    give[...] = jnp.where(first, whole_b, whole_a).astype(bf16)


def terms(acts, g_head, g_tail, table, at_a, at_b, arrived=(), last=False):
    head_depth, features = g_head.shape
    tail_depth = g_tail.shape[0]
    chunk = acts[0].shape[0] // 4
    left = [
        pl.BlockSpec((chunk, head_depth), lambda t, p: (p[at_a], 0)),
        pl.BlockSpec((chunk, tail_depth), lambda t, p: (p[at_a], 0)),
        pl.BlockSpec((chunk, head_depth), lambda t, p: (p[at_b], 0)),
        pl.BlockSpec((chunk, tail_depth), lambda t, p: (p[at_b], 0)),
    ]
    block = pl.BlockSpec((chunk, COLS), lambda t, p: (0, t))
    depth = head_depth + tail_depth
    return call(
        last_terms_body if last else functools.partial(terms_body, bool(arrived)),
        "last_terms" if last else "terms",
        (features // COLS,),
        1,
        left
        + [
            pl.BlockSpec((head_depth, COLS), lambda t, p: (0, t)),
            pl.BlockSpec((tail_depth, COLS), lambda t, p: (0, t)),
        ]
        + [block] * len(arrived),
        [block, block],
        [
            jax.ShapeDtypeStruct((chunk, features), f32 if last else bf16),
            jax.ShapeDtypeStruct((chunk, features), bf16),
        ],
        4 * chunk * depth * features,
        2 * (2 * chunk * depth + depth * features + 4 * chunk * features),
    )(table, *acts, g_head, g_tail, *arrived)


def shards(preact, grad_output, down_weight):
    gy = lax.axis_index("gy")
    gz = lax.axis_index("gz")
    gx = lax.axis_index("gx")
    y, h = gx % 4, gx // 4
    entries = [gy ^ j for j in range(4)]
    entries += [(gz + 2) % 4 ^ gy, (gz + 1) % 4 ^ gy, (gz + 3) % 4 ^ gy, gz ^ gy, gz]
    entries += [(y + 2) % 4, (y + 1) % 4, (y + 3) % 4, y, h, 0, 0]
    table = jnp.stack([jnp.asarray(entry, jnp.int32) for entry in entries])

    other_chip, other_core = gy_move(1, 0), gy_move(0, 1)
    z_up, z_down = gz_ring(1), gz_ring(-1)
    y_up, y_down = gx_move(0, 1), gx_move(0, -1)

    own, own_tail = grad_output[:HEAD], grad_output[HEAD:]
    across = lax.ppermute(own, "gy", other_chip)
    partner = lax.ppermute(own, "gy", other_core)
    partner_tail = lax.ppermute(own_tail, "gy", other_core)

    acts = transposed_gelu(preact, table, 0)
    table = after(table, *acts)

    corner = lax.ppermute(after(across, table), "gy", other_core)
    across_tail = lax.ppermute(after(own_tail, across, table), "gy", other_chip)
    head = jnp.stack((own, partner, across, corner))

    a_far, b_far = head_parts(head, down_weight, table, FAR, FAR)
    table = after(table, a_far)
    a_far = lax.ppermute(a_far, "gz", z_down)
    b_far = lax.ppermute(b_far, "gz", z_up)
    a_side, b_side = head_parts(head, down_weight, table, UP, DOWN)
    table = after(table, a_side)
    a_side = lax.ppermute(a_side, "gz", z_up)
    b_side = lax.ppermute(b_side, "gz", z_down)

    more = transposed_gelu(preact, table, 1)
    acts = [*acts, *more]
    table = after(table, *more)

    a_sum, b_sum = head_parts(head, down_weight, table, DOWN, UP, a_far, b_far)
    table = after(table, a_sum)
    a_sum = lax.ppermute(a_sum, "gz", z_down)
    b_sum = lax.ppermute(b_sum, "gz", z_up)

    table = after(table, a_side, b_side)
    corner_tail = lax.ppermute(after(across_tail, table), "gy", other_core)
    tail = jnp.stack((own_tail, partner_tail, across_tail, corner_tail))
    part = tail_parts(tail, down_weight, table)
    table = after(table, part)
    summed = lax.psum_scatter(
        part.reshape(-1, part.shape[2]), "gz", scatter_dimension=0, tiled=True
    )

    g_head = head.reshape(-1, head.shape[2])
    g_tail = tail.reshape(-1, tail.shape[2])
    c_far, d_far = terms(acts, g_head, g_tail, table, Y_FAR, Y_FAR)
    table = after(table, c_far)
    c_far = lax.ppermute(c_far, "gx", y_down)
    d_far = lax.ppermute(d_far, "gx", y_up)
    c_side, d_side = terms(acts, g_head, g_tail, table, Y_UP, Y_DOWN)
    table = after(table, c_side)
    c_side = lax.ppermute(c_side, "gx", y_up)
    d_side = lax.ppermute(d_side, "gx", y_down)

    held = head_last(head, down_weight, preact, table, a_side, a_sum, b_side, b_sum)
    table = after(table, held)

    c_sum, d_sum = terms(acts, g_head, g_tail, table, Y_DOWN, Y_UP, (c_far, d_far))
    table = after(table, c_sum)
    c_sum = lax.ppermute(c_sum, "gx", y_down)
    d_sum = lax.ppermute(d_sum, "gx", y_up)
    keep, give = terms(
        acts, g_head, g_tail, table, Y, Y, (c_side, c_sum, d_side, d_sum), last=True
    )
    taken = lax.ppermute(give, "gx", gx_move(1, 0))
    grad_down = (keep + taken.astype(f32)).astype(bf16)

    grad_pre = tail_last(summed, preact, table, held)
    return (grad_pre, grad_down)


def solution(mesh):
    return jax.shard_map(
        shards,
        mesh=mesh,
        in_specs=(P("gx", "gy"), P(("gx", "gy"), "gz"), P("gy", "gz")),
        out_specs=(P(("gx", "gz"), "gy"), P(("gy", "gx"), "gz")),
        check_vma=False,
    )
```

```python
import functools
import math

import jax
import jax.numpy as jnp
from jax import lax
from jax.experimental import pallas as pl
from jax.experimental.pallas import tpu as pltpu
from jax.sharding import PartitionSpec as P

root_half = 1.0 / math.sqrt(2.0)
slope_scale = 1.0 / math.sqrt(2.0 * math.pi)
bf16 = jnp.bfloat16
f32 = jnp.float32
HEAD = 128
TILE = 512
STEP = 256
Y_FIRST = 640
SHORT, LONG = 1 / 64, 512
VMEM = 63 * 1024 * 1024


def gelu(values):
    return 0.5 * values * (1.0 + lax.erf(values * root_half))


def unit_slope(values):
    return (
        0.5 * (1.0 + lax.erf(values * root_half))
        + values * jnp.exp(-0.5 * values * values) * slope_scale
    )


def gz_ring(step):
    return [(i, (i + step) % 4) for i in range(4)]


def gx_move(dh, dy):
    return [(h * 4 + y, (h + dh) % 2 * 4 + (y + dy) % 4) for h in range(2) for y in range(4)]


def gy_move(dl, dc):
    return [(l * 2 + c, (l + dl) % 2 * 2 + (c + dc) % 2) for l in range(2) for c in range(2)]


def after(value, *others):
    return lax.optimization_barrier((value,) + others)[0]


def call(body, name, grid, prefetch, in_specs, out_specs, out_shape, flops, moved, scratch=(), cost=1, aliases=None):
    return pl.pallas_call(
        body,
        name=name,
        out_shape=out_shape,
        grid_spec=pltpu.PrefetchScalarGridSpec(
            num_scalar_prefetch=prefetch, grid=grid, in_specs=in_specs, out_specs=out_specs,
            scratch_shapes=list(scratch),
        ),
        compiler_params=pltpu.CompilerParams(
            dimension_semantics=("arbitrary",) * len(grid), vmem_limit_bytes=VMEM
        ),
        input_output_aliases=aliases or {},
        cost_estimate=pl.CostEstimate(
            flops=int(flops * cost), bytes_accessed=int(moved * cost), transcendentals=0
        ),
    )


def rows_dot(rows, weights):
    return lax.dot_general(rows, weights, (((1,), (1,)), ((), ())), preferred_element_type=f32)


def cols_dot(left, right):
    return lax.dot_general(left, right, (((0,), (0,)), ((), ())), preferred_element_type=f32)


ORDER, FAR, UP, DOWN, OWN, GZ, H = 0, 4, 5, 6, 7, 8, 9


def first_body(table, rows, weights, out):
    part = rows_dot(rows[...], weights[...]).astype(bf16)
    count = out.shape[1]
    for j in range(4):
        out[table[ORDER + j]] = part[j * count : (j + 1) * count]


def first_parts(rows, weights, table):
    _, count, depth = rows.shape
    hidden = weights.shape[0]
    return call(
        first_body,
        "first_parts",
        (hidden // TILE,),
        1,
        [
            pl.BlockSpec((4 * count, depth), lambda t, o: (0, 0)),
            pl.BlockSpec((TILE, depth), lambda t, o: (t, 0)),
        ],
        pl.BlockSpec((4, count, TILE), lambda t, o: (0, 0, t)),
        jax.ShapeDtypeStruct((4, count, hidden), bf16),
        8 * count * depth * hidden,
        2 * (4 * count * depth + depth * hidden + 4 * count * hidden),
    )(table, rows.reshape(4 * count, depth), weights)


def pair_body(adds, table, rows_a, rows_b, weights_a, weights_b, *refs):
    out_a, out_b = refs[-2:]
    sum_a = rows_dot(rows_a[0], weights_a[...])
    sum_b = rows_dot(rows_b[0], weights_b[...])
    if adds:
        sum_a += refs[0][...].astype(f32)
        sum_b += refs[1][...].astype(f32)
    out_a[...] = sum_a.astype(bf16)
    out_b[...] = sum_b.astype(bf16)


def pair_parts(rows, weights, table, at_a, at_b, *arrived):
    _, count, depth = rows.shape
    hidden = weights.shape[0]
    tiles = hidden // 2 // STEP
    half = pl.BlockSpec((count, STEP), lambda t, p: (0, t))
    shape = jax.ShapeDtypeStruct((count, hidden // 2), bf16)
    return call(
        functools.partial(pair_body, bool(arrived)),
        "pair_parts",
        (tiles,),
        1,
        [
            pl.BlockSpec((1, count, depth), lambda t, p: (p[at_a], 0, 0)),
            pl.BlockSpec((1, count, depth), lambda t, p: (p[at_b], 0, 0)),
            pl.BlockSpec((STEP, depth), lambda t, p: (t, 0)),
            pl.BlockSpec((STEP, depth), lambda t, p: (tiles + t, 0)),
        ]
        + [half] * len(arrived),
        [half, half],
        [shape, shape],
        2 * count * depth * hidden,
        2 * (2 * count * depth + depth * hidden + count * hidden * (1 + len(arrived) // 2)),
        cost=SHORT,
    )(table, rows, rows, weights, weights, *arrived)


def own_body(table, rows, weights, pre, side_a, sum_a, side_b, sum_b, held, out):
    total = rows_dot(rows[0], weights[...])
    slope = unit_slope(pre[...].astype(f32))
    first = pl.program_id(0) < pl.num_programs(0) // 2
    head = out.shape[0] - total.shape[0]
    out[:head] = held[...]

    @pl.when(first)
    def _():
        whole = total + side_a[...].astype(f32) + sum_a[...].astype(f32)
        out[head:] = (whole * slope[head:]).astype(bf16)

    @pl.when(jnp.logical_not(first))
    def _():
        whole = total + side_b[...].astype(f32) + sum_b[...].astype(f32)
        out[head:] = (whole * slope[head:]).astype(bf16)


def own_rows(rows, weights, preact, table, side_a, sum_a, side_b, sum_b, held):
    share = preact.shape[0] // 4
    _, count, depth = rows.shape
    hidden = weights.shape[0]
    tiles = hidden // TILE
    half_a = pl.BlockSpec((count, TILE), lambda t, p: (0, jnp.minimum(t, tiles // 2 - 1)))
    half_b = pl.BlockSpec((count, TILE), lambda t, p: (0, jnp.maximum(t - tiles // 2, 0)))
    return call(
        own_body,
        "own_rows",
        (tiles,),
        1,
        [
            pl.BlockSpec((1, count, depth), lambda t, p: (p[OWN], 0, 0)),
            pl.BlockSpec((TILE, depth), lambda t, p: (t, 0)),
            pl.BlockSpec((share, TILE), lambda t, p: (p[GZ], t)),
            half_a,
            half_a,
            half_b,
            half_b,
            pl.BlockSpec((share - count, TILE), lambda t, p: (0, t)),
        ],
        pl.BlockSpec((share, TILE), lambda t, p: (0, t)),
        jax.ShapeDtypeStruct((share, hidden), bf16),
        2 * count * depth * hidden,
        2 * (count * depth + depth * hidden + 4 * count * hidden),
        cost=LONG,
    )(table, rows, weights, preact, side_a, sum_a, side_b, sum_b, held)


def sloped_body(table, summed, pre, out):
    out[...] = (summed[...].astype(f32) * unit_slope(pre[...].astype(f32))).astype(bf16)


def sloped(summed, preact, table):
    count, hidden = summed.shape
    share = preact.shape[0] // 4
    width = hidden // 2
    return call(
        sloped_body,
        "sloped",
        (2,),
        1,
        [
            pl.BlockSpec((count, width), lambda t, p: (0, t)),
            pl.BlockSpec((count, width), lambda t, p: (p[GZ] * (share // count), t)),
        ],
        pl.BlockSpec((count, width), lambda t, p: (0, t)),
        jax.ShapeDtypeStruct((count, hidden), bf16),
        count * hidden * 40,
        6 * count * hidden,
        cost=LONG,
    )(table, summed, preact)


def near_body(table, pre_own, pre_partner, own, partner, *refs):
    total = cols_dot(gelu(pre_own[...].astype(f32)).astype(bf16), own[...])
    total += cols_dot(gelu(pre_partner[...].astype(f32)).astype(bf16), partner[...])
    refs[-1][...] = total


def near_terms(preact, own, partner, table, *held):
    rows, hidden = preact.shape
    share, features = own.shape
    chunk = hidden // 8
    start = 4 if held else 0
    return call(
        near_body,
        "near_terms",
        (4,),
        1,
        [
            pl.BlockSpec((share, chunk), lambda t, p: (p[ORDER], start + t)),
            pl.BlockSpec((share, chunk), lambda t, p: (p[ORDER + 1], start + t)),
            pl.BlockSpec((share, features), lambda t, p: (0, 0)),
            pl.BlockSpec((share, features), lambda t, p: (0, 0)),
        ]
        + [pl.BlockSpec(memory_space=pl.ANY)] * len(held),
        pl.BlockSpec((chunk, features), lambda t, p: (start + t, 0)),
        jax.ShapeDtypeStruct((hidden, features), f32),
        2 * share * features * hidden,
        share * hidden + 2 * share * features + 2 * features * hidden,
        cost=LONG if held else SHORT,
        aliases={5: 0} if held else {},
    )(table, preact, preact, own, partner, *held)


def far_body(table, pre_a, pre_b, head, tail, held, y_first, give, keep, rows):
    share = pre_a.shape[0]
    count = head.shape[1]

    @pl.when(pl.program_id(0) == 0)
    def _():
        for j in range(2):
            rows[j * share : j * share + count] = head[j]
            rows[j * share + count : (j + 1) * share] = tail[j]

    total = held[...]
    total += cols_dot(gelu(pre_a[...].astype(f32)).astype(bf16), rows[:share])
    total += cols_dot(gelu(pre_b[...].astype(f32)).astype(bf16), rows[share:])
    total = total.astype(bf16)
    split = y_first.shape[1]
    y_first[...] = total[:, :split]

    @pl.when(pl.program_id(0) < 4)
    def _():
        give[...] = total[:, split:]

    @pl.when(pl.program_id(0) >= 4)
    def _():
        keep[...] = total[:, split:]


def far_terms(preact, head, tail, held, table):
    rows, hidden = preact.shape
    features = held.shape[1]
    share = rows // 4
    chunk = hidden // 8
    rest = features - Y_FIRST

    def half(t, p):
        return (p[H] + 1 + t // 4) % 2

    def source(t, p):
        return half(t, p) * 4 + t % 4

    return call(
        far_body,
        "far_terms",
        (8,),
        1,
        [
            pl.BlockSpec((share, chunk), lambda t, p: (p[ORDER + 2], source(t, p))),
            pl.BlockSpec((share, chunk), lambda t, p: (p[ORDER + 3], source(t, p))),
            pl.BlockSpec((2, head.shape[1], features), lambda t, p: (1, 0, 0)),
            pl.BlockSpec((2, tail.shape[1], features), lambda t, p: (1, 0, 0)),
            pl.BlockSpec((chunk, features), lambda t, p: (source(t, p), 0)),
        ],
        [
            pl.BlockSpec((chunk, Y_FIRST), lambda t, p: (t % 4 * 2 + half(t, p), 0)),
            pl.BlockSpec((chunk, rest), lambda t, p: (jnp.minimum(t, 3), 0)),
            pl.BlockSpec((chunk, rest), lambda t, p: (jnp.maximum(t - 4, 0), 0)),
        ],
        [
            jax.ShapeDtypeStruct((hidden, Y_FIRST), bf16),
            jax.ShapeDtypeStruct((hidden // 2, rest), bf16),
            jax.ShapeDtypeStruct((hidden // 2, rest), bf16),
        ],
        4 * share * features * hidden,
        2 * (2 * share * hidden + 2 * share * features + 3 * features * hidden),
        scratch=[pltpu.VMEM((2 * share, features), bf16)],
        cost=SHORT,
    )(table, preact, preact, head, tail, held)


def shards(preact, grad_output, down_weight):
    gy = lax.axis_index("gy")
    gz = lax.axis_index("gz")
    gx = lax.axis_index("gx")
    y, h = gx % 4, gx // 4
    entries = [gy ^ j for j in range(4)]
    entries += [(gz + 2) % 4 ^ gy, (gz + 1) % 4 ^ gy, (gz + 3) % 4 ^ gy, gz ^ gy, gz, h, 0, 0]
    table = jnp.stack([jnp.asarray(entry, jnp.int32) for entry in entries])

    other_chip, other_core = gy_move(1, 0), gy_move(0, 1)
    z_up, z_down = gz_ring(1), gz_ring(-1)
    along_y = [[0, 1, 2, 3], [4, 5, 6, 7]]

    own_head, own_tail = grad_output[:HEAD], grad_output[HEAD:]
    across = lax.ppermute(own_head, "gy", other_chip)
    partner = lax.ppermute(grad_output, "gy", other_core)
    corner = lax.ppermute(across, "gy", other_core)
    across_tail = lax.ppermute(after(own_tail, across), "gy", other_chip)

    head = jnp.stack((own_head, partner[:HEAD], across, corner))
    parts = first_parts(head, down_weight, table)
    table = after(table, parts)
    summed = lax.psum_scatter(
        parts.reshape(-1, parts.shape[2]), "gz", scatter_dimension=0, tiled=True
    )

    near = near_terms(preact, grad_output, partner, table)
    table = after(table, near)
    corner_tail = lax.ppermute(after(across_tail, table), "gy", other_core)
    near = near_terms(preact, grad_output, partner, table, near)
    table = after(table, near)

    tail = jnp.stack((own_tail, partner[HEAD:], across_tail, corner_tail))
    a_far, b_far = pair_parts(tail, down_weight, table, FAR, FAR)
    table = after(table, a_far)
    a_far = lax.ppermute(a_far, "gz", z_down)
    b_far = lax.ppermute(b_far, "gz", z_up)

    y_first, give, keep = far_terms(preact, head, tail, near, table)
    table = after(table, y_first)
    taken = lax.ppermute(give, "gx", gx_move(1, 0))
    y_first = lax.psum_scatter(
        y_first, "gx", scatter_dimension=0, axis_index_groups=along_y, tiled=True
    )

    a_side, b_side = pair_parts(tail, down_weight, table, UP, DOWN)
    table = after(table, a_side)
    a_side = lax.ppermute(after(a_side, a_far, b_far), "gz", z_up)
    b_side = lax.ppermute(after(b_side, a_far, b_far), "gz", z_down)

    a_sum, b_sum = pair_parts(tail, down_weight, table, DOWN, UP, a_far, b_far)
    table = after(table, a_sum)
    a_sum = lax.ppermute(a_sum, "gz", z_down)
    b_sum = lax.ppermute(b_sum, "gz", z_up)

    held = sloped(summed, preact, after(table, a_side, b_side))
    table = after(table, held)

    both = (keep.astype(f32) + after(taken, table).astype(f32)).astype(bf16)
    x_first = lax.psum_scatter(
        after(both, y_first), "gx", scatter_dimension=0, axis_index_groups=along_y, tiled=True
    )
    table = after(table, both)

    mine, other = jnp.split(after(y_first, table), 2)
    mine, other = jnp.where(h == 0, mine, other), jnp.where(h == 0, other, mine)
    crossed = lax.ppermute(other, "gx", gx_move(1, 0))

    grad_pre = own_rows(
        tail, down_weight, preact, table, a_side, a_sum, b_side, b_sum, held
    )
    y_first = (mine.astype(f32) + crossed.astype(f32)).astype(bf16)
    grad_down = jnp.concatenate((y_first, x_first), axis=1)
    return (grad_pre, grad_down)


def solution(mesh):
    return jax.shard_map(
        shards,
        mesh=mesh,
        in_specs=(P("gx", "gy"), P(("gx", "gy"), "gz"), P("gy", "gz")),
        out_specs=(P(("gx", "gz"), "gy"), P(("gy", "gx"), "gz")),
        check_vma=False,
    )
```

```python
import functools
import math

import jax
import jax.numpy as jnp
from jax import lax
from jax.experimental import pallas as pl
from jax.experimental.pallas import tpu as pltpu
from jax.sharding import PartitionSpec as P

root_half = 1.0 / math.sqrt(2.0)
slope_scale = 1.0 / math.sqrt(2.0 * math.pi)
bf16 = jnp.bfloat16
f32 = jnp.float32
HEAD = 128
TILE = 512
SHORT, SIDE, LAST, LONG = 1 / 64, 1 / 64, 2, 512
VMEM = 63 * 1024 * 1024


def gelu(values):
    return 0.5 * values * (1.0 + lax.erf(values * root_half))


def unit_slope(values):
    return (
        0.5 * (1.0 + lax.erf(values * root_half))
        + values * jnp.exp(-0.5 * values * values) * slope_scale
    )


def gz_ring(step):
    return [(i, (i + step) % 4) for i in range(4)]


def gx_move(dh, dy):
    return [(h * 4 + y, (h + dh) % 2 * 4 + (y + dy) % 4) for h in range(2) for y in range(4)]


def gy_move(dl, dc):
    return [(l * 2 + c, (l + dl) % 2 * 2 + (c + dc) % 2) for l in range(2) for c in range(2)]


def after(value, *others):
    return lax.optimization_barrier((value,) + others)[0]


def call(body, name, grid, prefetch, in_specs, out_specs, out_shape, flops, moved, scratch=(), cost=1, aliases=None):
    return pl.pallas_call(
        body,
        name=name,
        out_shape=out_shape,
        grid_spec=pltpu.PrefetchScalarGridSpec(
            num_scalar_prefetch=prefetch, grid=grid, in_specs=in_specs, out_specs=out_specs,
            scratch_shapes=list(scratch),
        ),
        compiler_params=pltpu.CompilerParams(
            dimension_semantics=("arbitrary",) * len(grid), vmem_limit_bytes=VMEM
        ),
        input_output_aliases=aliases or {},
        cost_estimate=pl.CostEstimate(
            flops=int(flops * cost), bytes_accessed=int(moved * cost), transcendentals=0
        ),
    )


def rows_dot(rows, weights):
    return lax.dot_general(rows, weights, (((1,), (1,)), ((), ())), preferred_element_type=f32)


def cols_dot(left, right):
    return lax.dot_general(left, right, (((0,), (0,)), ((), ())), preferred_element_type=f32)


ORDER, FAR, UP, DOWN, OWN, GZ = 0, 4, 5, 6, 7, 8
C_FAR, C_SIDE, C_SUM, C_OWN = 10, 12, 14, 16


def first_body(table, rows, weights, up, down, far, own, part):
    count = up.shape[0]
    total = rows_dot(rows[...], weights[...]).astype(bf16)
    for j in range(4):
        part[j] = total[j * count : (j + 1) * count]
    up[...] = part[table[UP]]
    down[...] = part[table[DOWN]]
    far[...] = part[table[FAR]]
    own[...] = part[table[OWN]]


def first_parts(rows, weights, table):
    _, count, depth = rows.shape
    hidden = weights.shape[0]
    block = pl.BlockSpec((count, TILE), lambda t, o: (0, t))
    return call(
        first_body,
        "first_parts",
        (hidden // TILE,),
        1,
        [
            pl.BlockSpec((4 * count, depth), lambda t, o: (0, 0)),
            pl.BlockSpec((TILE, depth), lambda t, o: (t, 0)),
        ],
        [block] * 4,
        [jax.ShapeDtypeStruct((count, hidden), bf16)] * 4,
        8 * count * depth * hidden,
        2 * (4 * count * depth + depth * hidden + 4 * count * hidden),
        scratch=[pltpu.VMEM((4, count, TILE), bf16)],
        cost=SHORT,
    )(table, rows.reshape(4 * count, depth), weights)


def tail_body(table, rows, weights, far_a, far_b, side_a, side_b, sum_a, sum_b, own, left, part):
    count = own.shape[0]
    first = pl.program_id(0) < pl.num_programs(0) // 2

    @pl.when(pl.program_id(0) == 0)
    def _():
        for j in range(4):
            left[j * count : (j + 1) * count] = rows[j, HEAD:]

    total = rows_dot(left[...], weights[...]).astype(bf16)
    for j in range(4):
        part[j] = total[j * count : (j + 1) * count]
    own[...] = part[table[OWN]]

    @pl.when(first)
    def _():
        far_a[...] = part[table[FAR]]
        side_a[...] = part[table[UP]]
        sum_a[...] = part[table[DOWN]]

    @pl.when(jnp.logical_not(first))
    def _():
        far_b[...] = part[table[FAR]]
        side_b[...] = part[table[DOWN]]
        sum_b[...] = part[table[UP]]


def tail_parts(rows, weights, table):
    _, share, depth = rows.shape
    count = share - HEAD
    hidden = weights.shape[0]
    tiles = hidden // TILE
    half_a = pl.BlockSpec((count, TILE), lambda t, p: (0, jnp.minimum(t, tiles // 2 - 1)))
    half_b = pl.BlockSpec((count, TILE), lambda t, p: (0, jnp.maximum(t - tiles // 2, 0)))
    half = jax.ShapeDtypeStruct((count, hidden // 2), bf16)
    return call(
        tail_body,
        "tail_parts",
        (tiles,),
        1,
        [
            pl.BlockSpec((4, share, depth), lambda t, o: (0, 0, 0)),
            pl.BlockSpec((TILE, depth), lambda t, o: (t, 0)),
        ],
        [half_a, half_b] * 3 + [pl.BlockSpec((count, TILE), lambda t, o: (0, t))],
        [half] * 6 + [jax.ShapeDtypeStruct((count, hidden), bf16)],
        8 * count * depth * hidden,
        2 * (4 * share * depth + depth * hidden + 4 * count * hidden),
        scratch=[pltpu.VMEM((4 * count, depth), bf16), pltpu.VMEM((4, count, TILE), bf16)],
        cost=SHORT,
    )(table, rows, weights)


def head_last_body(table, own, one, two, three, pre, out):
    total = own[...].astype(f32) + one[...].astype(f32)
    total += two[...].astype(f32) + three[...].astype(f32)
    out[...] = (total * unit_slope(pre[...].astype(f32))).astype(bf16)


def head_last(own, arrived, preact, table):
    count, hidden = own.shape
    share = preact.shape[0] // 4
    width = hidden // 2
    block = pl.BlockSpec((count, width), lambda t, p: (0, t))
    return call(
        head_last_body,
        "head_last",
        (2,),
        1,
        [block] * 4
        + [pl.BlockSpec((count, width), lambda t, p: (p[GZ] * (share // count), t))],
        block,
        jax.ShapeDtypeStruct((share, hidden), bf16),
        count * hidden * 40,
        12 * count * hidden,
        cost=LONG,
    )(table, own, *arrived, preact)


def tail_last_body(table, own, side_a, sum_a, side_b, sum_b, pre, held, out):
    width = side_a.shape[1]
    slope = unit_slope(pre[...].astype(f32))
    total = own[...].astype(f32)
    first = total[:, :width] + side_a[...].astype(f32) + sum_a[...].astype(f32)
    second = total[:, width:] + side_b[...].astype(f32) + sum_b[...].astype(f32)
    out[:, :width] = (first * slope[:, :width]).astype(bf16)
    out[:, width:] = (second * slope[:, width:]).astype(bf16)


def tail_last(own, side_a, sum_a, side_b, sum_b, preact, table, held):
    count, hidden = own.shape
    share = preact.shape[0] // 4
    step = 128
    start, blocks = HEAD // step, share // step
    half = pl.BlockSpec((step, hidden // 2), lambda t, p: (t, 0))
    return call(
        tail_last_body,
        "tail_last",
        (count // step,),
        1,
        [
            pl.BlockSpec((step, hidden), lambda t, p: (t, 0)),
            half,
            half,
            half,
            half,
            pl.BlockSpec((step, hidden), lambda t, p: (p[GZ] * blocks + start + t, 0)),
            pl.BlockSpec(memory_space=pl.ANY),
        ],
        pl.BlockSpec((step, hidden), lambda t, p: (start + t, 0)),
        jax.ShapeDtypeStruct((share, hidden), bf16),
        count * hidden * 40,
        10 * count * hidden,
        aliases={7: 0},
    )(table, own, side_a, sum_a, side_b, sum_b, preact, held)


def near_body(table, pre_own, pre_partner, own, partner, out):
    total = cols_dot(gelu(pre_own[...].astype(f32)).astype(bf16), own[...])
    total += cols_dot(gelu(pre_partner[...].astype(f32)).astype(bf16), partner[...])
    out[0] = total.astype(bf16)


def near_terms(preact, own, partner, table, at, cost=SHORT):
    rows, hidden = preact.shape
    share, features = own.shape
    chunk = hidden // 8
    return call(
        near_body,
        "near_terms",
        (2,),
        1,
        [
            pl.BlockSpec((share, chunk), lambda t, p: (p[ORDER], p[at + t])),
            pl.BlockSpec((share, chunk), lambda t, p: (p[ORDER + 1], p[at + t])),
            pl.BlockSpec((share, features), lambda t, p: (0, 0)),
            pl.BlockSpec((share, features), lambda t, p: (0, 0)),
        ],
        pl.BlockSpec((1, chunk, features), lambda t, p: (t, 0, 0)),
        jax.ShapeDtypeStruct((2, chunk, features), bf16),
        8 * share * features * chunk,
        2 * (4 * share * chunk + 2 * share * features + 2 * features * chunk),
        cost=cost,
    )(table, preact, preact, own, partner)


def terms_body(near, table, *refs):
    extra = refs[-4] if near else None
    rows, out_a, out_b = refs[-3:]
    total = None
    share = refs[0].shape[0]
    for j, pre in enumerate(refs[: 2 if near else 4]):
        act = gelu(pre[...].astype(f32)).astype(bf16)
        term = cols_dot(act, rows[j])
        total = term if total is None else total + term
    if near:
        total += extra[0].astype(f32)

    @pl.when(pl.program_id(0) == 0)
    def _():
        out_a[...] = total.astype(bf16)

    @pl.when(pl.program_id(0) == 1)
    def _():
        out_b[...] = total.astype(bf16)


def terms(preact, rows, table, at, held=None, cost=SHORT):
    hidden = preact.shape[1]
    _, share, features = rows.shape
    chunk = hidden // 8
    near = held is not None
    pieces = (2, 3) if near else (0, 1, 2, 3)

    def source(j):
        return pl.BlockSpec((share, chunk), lambda t, p: (p[ORDER + j], p[at + t]))

    out = pl.BlockSpec((chunk, features), lambda t, p: (0, 0))
    return call(
        functools.partial(terms_body, near),
        "terms",
        (2,),
        1,
        [source(j) for j in pieces]
        + [pl.BlockSpec((1, chunk, features), lambda t, p: (t, 0, 0))] * near
        + [pl.BlockSpec((len(pieces), share, features), lambda t, p: (int(near), 0, 0))],
        [out, out],
        [jax.ShapeDtypeStruct((chunk, features), bf16)] * 2,
        4 * len(pieces) * share * features * chunk,
        2 * (2 * len(pieces) * share * chunk + len(pieces) * share * features),
        cost=cost,
    )(table, *[preact] * len(pieces), *([held] if near else []), rows)


def shards(preact, grad_output, down_weight):
    gy = lax.axis_index("gy")
    gz = lax.axis_index("gz")
    gx = lax.axis_index("gx")
    y, h = gx % 4, gx // 4
    entries = [gy ^ j for j in range(4)]
    entries += [(gz + 2) % 4 ^ gy, (gz + 1) % 4 ^ gy, (gz + 3) % 4 ^ gy, gz ^ gy, gz, 0]
    up, down, far = (y + 1) % 4, (y + 3) % 4, (y + 2) % 4
    entries += [far, 4 + far, up, 4 + down, down, 4 + up, y, 4 + y]
    table = jnp.stack([jnp.asarray(entry, jnp.int32) for entry in entries])

    other_chip, other_core = gy_move(1, 0), gy_move(0, 1)
    z_up, z_down, z_far = gz_ring(1), gz_ring(-1), gz_ring(2)
    y_up, y_down = gx_move(0, 1), gx_move(0, -1)

    def add(*values):
        return sum(value.astype(f32) for value in values)

    own_head, own_tail = grad_output[:HEAD], grad_output[HEAD:]
    across = lax.ppermute(own_head, "gy", other_chip)
    partner = lax.ppermute(grad_output, "gy", other_core)
    near_far = near_terms(preact, grad_output, partner, table, C_FAR)
    table = after(table, near_far)
    corner = lax.ppermute(after(across, table), "gy", other_core)
    across_tail = lax.ppermute(after(own_tail, across, table), "gy", other_chip)

    head = jnp.stack((own_head, partner[:HEAD], across, corner))
    to_up, to_down, to_far, own = first_parts(head, down_weight, table)
    table = after(table, own)
    arrived = [
        lax.ppermute(to_up, "gz", z_up),
        lax.ppermute(to_down, "gz", z_down),
        lax.ppermute(to_far, "gz", z_far),
    ]

    near_side = near_terms(preact, grad_output, partner, table, C_SIDE)
    table = after(table, near_side)
    across_tail = after(across_tail, table)
    corner_tail = [
        lax.ppermute(across_tail[start : start + 96], "gy", other_core)
        for start in range(0, across_tail.shape[0], 96)
    ]
    rows = jnp.stack(
        (
            grad_output,
            partner,
            lax.optimization_barrier(jnp.concatenate((across, across_tail))),
            lax.optimization_barrier(jnp.concatenate((corner, *corner_tail))),
        )
    )

    c_far, d_far = terms(preact, rows, table, C_FAR, near_far)
    table = after(table, c_far)
    c_far = lax.ppermute(c_far, "gx", y_down)
    d_far = lax.ppermute(d_far, "gx", y_up)

    a_far, b_far, a_side, b_side, a_sum, b_sum, own_tail = tail_parts(rows, down_weight, table)
    table = after(table, own_tail)
    a_far = lax.ppermute(after(a_far, *arrived), "gz", z_down)
    b_far = lax.ppermute(after(b_far, *arrived), "gz", z_up)
    table = after(table, *arrived)

    c_side, d_side = terms(preact, rows, table, C_SIDE, near_side, cost=SIDE)
    table = after(table, c_side)
    c_side = lax.ppermute(after(c_side, c_far, d_far), "gx", y_up)
    d_side = lax.ppermute(after(d_side, c_far, d_far), "gx", y_down)

    c_sum, d_sum = terms(preact, rows, table, C_SUM)
    table = after(table, c_sum)
    c_own, d_own = terms(preact, rows, table, C_OWN, cost=LAST)
    table = after(table, c_own)

    a_side = lax.ppermute(after(a_side, table, a_far, b_far), "gz", z_up)
    b_side = lax.ppermute(after(b_side, table, a_far, b_far), "gz", z_down)
    c_sum = lax.ppermute(after(add(c_sum, c_far).astype(bf16), table, c_side, d_side, a_far, b_far), "gx", y_down)
    d_sum = lax.ppermute(after(add(d_sum, d_far).astype(bf16), table, c_side, d_side, a_far, b_far), "gx", y_up)

    held = head_last(own, arrived, preact, table)
    table = after(table, held)

    a_sum = lax.ppermute(after(add(a_sum, a_far).astype(bf16), a_side, b_side), "gz", z_down)
    b_sum = lax.ppermute(after(add(b_sum, b_far).astype(bf16), a_side, b_side), "gz", z_up)

    c_sum, d_sum = after(c_sum, a_side, b_side), after(d_sum, a_side, b_side)
    c_own = add(after(c_own, a_side, b_side), c_side, c_sum)
    d_own = add(d_own, d_side, d_sum)
    keep = jnp.where(h == 0, c_own, d_own)
    give = jnp.where(h == 0, d_own, c_own).astype(bf16)
    taken = lax.ppermute(give, "gx", gx_move(1, 0))

    grad_pre = tail_last(own_tail, a_side, a_sum, b_side, b_sum, preact, table, held)
    grad_down = add(keep, taken).astype(bf16)
    return (grad_pre, grad_down)


def solution(mesh):
    return jax.shard_map(
        shards,
        mesh=mesh,
        in_specs=(P("gx", "gy"), P(("gx", "gy"), "gz"), P("gy", "gz")),
        out_specs=(P(("gx", "gz"), "gy"), P(("gy", "gx"), "gz")),
        check_vma=False,
    )
```

```python
import functools
import math

import jax
import jax.numpy as jnp
from jax import lax
from jax.experimental import pallas as pl
from jax.experimental.pallas import tpu as pltpu
from jax.sharding import PartitionSpec as P

root_half = 1.0 / math.sqrt(2.0)
slope_scale = 1.0 / math.sqrt(2.0 * math.pi)
bf16 = jnp.bfloat16
f32 = jnp.float32
HEAD = 192
TILE = 512
PIECE = 80
SHORT, MID, LAST, LONG = 1 / 64, 1/64, 1/64, 1/64
VMEM = 63 * 1024 * 1024


def gelu(values):
    return 0.5 * values * (1.0 + lax.erf(values * root_half))


def unit_slope(values):
    return (
        0.5 * (1.0 + lax.erf(values * root_half))
        + values * jnp.exp(-0.5 * values * values) * slope_scale
    )


def gz_ring(step):
    return [(i, (i + step) % 4) for i in range(4)]


def gx_move(dh, dy):
    return [(h * 4 + y, (h + dh) % 2 * 4 + (y + dy) % 4) for h in range(2) for y in range(4)]


def gy_move(dl, dc):
    return [(l * 2 + c, (l + dl) % 2 * 2 + (c + dc) % 2) for l in range(2) for c in range(2)]


def after(value, *others):
    return lax.optimization_barrier((value,) + others)[0]


def call(body, name, grid, prefetch, in_specs, out_specs, out_shape, flops, moved, scratch=(), cost=1, aliases=None):
    return pl.pallas_call(
        body,
        name=name,
        out_shape=out_shape,
        grid_spec=pltpu.PrefetchScalarGridSpec(
            num_scalar_prefetch=prefetch, grid=grid, in_specs=in_specs, out_specs=out_specs,
            scratch_shapes=list(scratch),
        ),
        compiler_params=pltpu.CompilerParams(
            dimension_semantics=("arbitrary",) * len(grid), vmem_limit_bytes=VMEM
        ),
        input_output_aliases=aliases or {},
        cost_estimate=pl.CostEstimate(
            flops=int(flops * cost), bytes_accessed=int(moved * cost), transcendentals=0
        ),
    )


def rows_dot(rows, weights):
    return lax.dot_general(rows, weights, (((1,), (1,)), ((), ())), preferred_element_type=f32)


def cols_dot(left, right):
    return lax.dot_general(left, right, (((0,), (0,)), ((), ())), preferred_element_type=f32)


ORDER, FAR, UP, DOWN, OWN, GZ = 0, 4, 5, 6, 7, 8
C_FAR, C_SIDE, C_SUM, C_OWN = 10, 12, 14, 16


def first_body(table, rows, weights, up, down, far, own, part):
    count = up.shape[0]
    total = rows_dot(rows[...], weights[...]).astype(bf16)
    for j in range(4):
        part[j] = total[j * count : (j + 1) * count]
    up[...] = part[table[UP]]
    down[...] = part[table[DOWN]]
    far[...] = part[table[FAR]]
    own[...] = part[table[OWN]]


def first_parts(rows, weights, table):
    _, count, depth = rows.shape
    hidden = weights.shape[0]
    block = pl.BlockSpec((count, TILE), lambda t, o: (0, t))
    return call(
        first_body,
        "first_parts",
        (hidden // TILE,),
        1,
        [
            pl.BlockSpec((4 * count, depth), lambda t, o: (0, 0)),
            pl.BlockSpec((TILE, depth), lambda t, o: (t, 0)),
        ],
        [block] * 4,
        [jax.ShapeDtypeStruct((count, hidden), bf16)] * 4,
        8 * count * depth * hidden,
        2 * (4 * count * depth + depth * hidden + 4 * count * hidden),
        scratch=[pltpu.VMEM((4, count, TILE), bf16)],
        cost=SHORT,
    )(table, rows.reshape(4 * count, depth), weights)


def tail_body(table, rows, weights, far_a, far_b, side_a, side_b, sum_a, sum_b, own, left, part):
    count = own.shape[0]
    first = pl.program_id(0) < pl.num_programs(0) // 2

    @pl.when(pl.program_id(0) == 0)
    def _():
        for j in range(4):
            left[j * count : (j + 1) * count] = rows[j, HEAD:]

    total = rows_dot(left[...], weights[...]).astype(bf16)
    for j in range(4):
        part[j] = total[j * count : (j + 1) * count]
    own[...] = part[table[OWN]]

    @pl.when(first)
    def _():
        far_a[...] = part[table[FAR]]
        side_a[...] = part[table[UP]]
        sum_a[...] = part[table[DOWN]]

    @pl.when(jnp.logical_not(first))
    def _():
        far_b[...] = part[table[FAR]]
        side_b[...] = part[table[DOWN]]
        sum_b[...] = part[table[UP]]


def tail_parts(rows, weights, table):
    _, share, depth = rows.shape
    count = share - HEAD
    hidden = weights.shape[0]
    tiles = hidden // TILE
    half_a = pl.BlockSpec((count, TILE), lambda t, p: (0, jnp.minimum(t, tiles // 2 - 1)))
    half_b = pl.BlockSpec((count, TILE), lambda t, p: (0, jnp.maximum(t - tiles // 2, 0)))
    half = jax.ShapeDtypeStruct((count, hidden // 2), bf16)
    return call(
        tail_body,
        "tail_parts",
        (tiles,),
        1,
        [
            pl.BlockSpec((4, share, depth), lambda t, o: (0, 0, 0)),
            pl.BlockSpec((TILE, depth), lambda t, o: (t, 0)),
        ],
        [half_a, half_b] * 3 + [pl.BlockSpec((count, TILE), lambda t, o: (0, t))],
        [half] * 6 + [jax.ShapeDtypeStruct((count, hidden), bf16)],
        8 * count * depth * hidden,
        2 * (4 * share * depth + depth * hidden + 4 * count * hidden),
        scratch=[pltpu.VMEM((4 * count, depth), bf16), pltpu.VMEM((4, count, TILE), bf16)],
        cost=SHORT,
    )(table, rows, weights)


def head_last_body(table, own, one, two, three, pre, out):
    total = own[...].astype(f32) + one[...].astype(f32)
    total += two[...].astype(f32) + three[...].astype(f32)
    out[...] = (total * unit_slope(pre[: own.shape[0]].astype(f32))).astype(bf16)


def head_last(own, arrived, preact, table):
    count, hidden = own.shape
    share = preact.shape[0] // 4
    width = hidden // 2
    block = pl.BlockSpec((count, width), lambda t, p: (0, t))
    return call(
        head_last_body,
        "head_last",
        (2,),
        1,
        [block] * 4
        + [pl.BlockSpec((share, width), lambda t, p: (p[GZ], t))],
        block,
        jax.ShapeDtypeStruct((share, hidden), bf16),
        count * hidden * 40,
        12 * count * hidden,
        cost=LONG,
    )(table, own, *arrived, preact)


def tail_last_body(table, own, side_a, sum_a, side_b, sum_b, pre, held, out):
    width = side_a.shape[1]
    slope = unit_slope(pre[...].astype(f32))
    total = own[...].astype(f32)
    first = total[:, :width] + side_a[...].astype(f32) + sum_a[...].astype(f32)
    second = total[:, width:] + side_b[...].astype(f32) + sum_b[...].astype(f32)
    out[:, :width] = (first * slope[:, :width]).astype(bf16)
    out[:, width:] = (second * slope[:, width:]).astype(bf16)


def tail_last(own, side_a, sum_a, side_b, sum_b, preact, table, held):
    count, hidden = own.shape
    share = preact.shape[0] // 4
    step = 64
    start, blocks = HEAD // step, share // step
    half = pl.BlockSpec((step, hidden // 2), lambda t, p: (t, 0))
    return call(
        tail_last_body,
        "tail_last",
        (count // step,),
        1,
        [
            pl.BlockSpec((step, hidden), lambda t, p: (t, 0)),
            half,
            half,
            half,
            half,
            pl.BlockSpec((step, hidden), lambda t, p: (p[GZ] * blocks + start + t, 0)),
            pl.BlockSpec(memory_space=pl.ANY),
        ],
        pl.BlockSpec((step, hidden), lambda t, p: (start + t, 0)),
        jax.ShapeDtypeStruct((share, hidden), bf16),
        count * hidden * 40,
        10 * count * hidden,
        aliases={7: 0},
    )(table, own, side_a, sum_a, side_b, sum_b, preact, held)


def near_body(table, pre_own, pre_partner, own, partner, out):
    total = cols_dot(gelu(pre_own[...].astype(f32)).astype(bf16), own[...])
    total += cols_dot(gelu(pre_partner[...].astype(f32)).astype(bf16), partner[...])
    out[0] = total.astype(bf16)


def near_terms(preact, own, partner, table, at, cost=SHORT):
    rows, hidden = preact.shape
    share, features = own.shape
    chunk = hidden // 8
    return call(
        near_body,
        "near_terms",
        (2,),
        1,
        [
            pl.BlockSpec((share, chunk), lambda t, p: (p[ORDER], p[at + t])),
            pl.BlockSpec((share, chunk), lambda t, p: (p[ORDER + 1], p[at + t])),
            pl.BlockSpec((share, features), lambda t, p: (0, 0)),
            pl.BlockSpec((share, features), lambda t, p: (0, 0)),
        ],
        pl.BlockSpec((1, chunk, features), lambda t, p: (t, 0, 0)),
        jax.ShapeDtypeStruct((2, chunk, features), bf16),
        8 * share * features * chunk,
        2 * (4 * share * chunk + 2 * share * features + 2 * features * chunk),
        cost=cost,
    )(table, preact, preact, own, partner)


def terms_body(near, table, *refs):
    extra = refs[-4] if near else None
    rows, out_a, out_b = refs[-3:]
    total = None
    share = refs[0].shape[0]
    for j, pre in enumerate(refs[: 2 if near else 4]):
        act = gelu(pre[...].astype(f32)).astype(bf16)
        term = cols_dot(act, rows[j])
        total = term if total is None else total + term
    if near:
        total += extra[0].astype(f32)

    @pl.when(pl.program_id(0) == 0)
    def _():
        out_a[...] = total.astype(bf16)

    @pl.when(pl.program_id(0) == 1)
    def _():
        out_b[...] = total.astype(bf16)


def terms(preact, rows, table, at, held=None, cost=SHORT):
    hidden = preact.shape[1]
    _, share, features = rows.shape
    chunk = hidden // 8
    near = held is not None
    pieces = (2, 3) if near else (0, 1, 2, 3)

    def source(j):
        return pl.BlockSpec((share, chunk), lambda t, p: (p[ORDER + j], p[at + t]))

    out = pl.BlockSpec((chunk, features), lambda t, p: (0, 0))
    return call(
        functools.partial(terms_body, near),
        "terms",
        (2,),
        1,
        [source(j) for j in pieces]
        + [pl.BlockSpec((1, chunk, features), lambda t, p: (t, 0, 0))] * near
        + [pl.BlockSpec((len(pieces), share, features), lambda t, p: (int(near), 0, 0))],
        [out, out],
        [jax.ShapeDtypeStruct((chunk, features), bf16)] * 2,
        4 * len(pieces) * share * features * chunk,
        2 * (2 * len(pieces) * share * chunk + len(pieces) * share * features),
        cost=cost,
    )(table, *[preact] * len(pieces), *([held] if near else []), rows)


def shards(preact, grad_output, down_weight):
    gy = lax.axis_index("gy")
    gz = lax.axis_index("gz")
    gx = lax.axis_index("gx")
    y, h = gx % 4, gx // 4
    entries = [gy ^ j for j in range(4)]
    entries += [(gz + 2) % 4 ^ gy, (gz + 1) % 4 ^ gy, (gz + 3) % 4 ^ gy, gz ^ gy, gz, 0]
    up, down, far = (y + 1) % 4, (y + 3) % 4, (y + 2) % 4
    entries += [far, 4 + far, up, 4 + down, down, 4 + up, y, 4 + y]
    table = jnp.stack([jnp.asarray(entry, jnp.int32) for entry in entries])

    other_chip, other_core = gy_move(1, 0), gy_move(0, 1)
    z_up, z_down, z_far = gz_ring(1), gz_ring(-1), gz_ring(2)
    y_up, y_down = gx_move(0, 1), gx_move(0, -1)

    def add(*values):
        return sum(value.astype(f32) for value in values)

    own_head, own_tail = grad_output[:HEAD], grad_output[HEAD:]
    across = lax.ppermute(own_head, "gy", other_chip)
    partner = lax.ppermute(grad_output, "gy", other_core)
    near_far = near_terms(preact, grad_output, partner, table, C_FAR)
    table = after(table, near_far)
    corner = lax.ppermute(after(across, table), "gy", other_core)
    across_tail = lax.ppermute(after(own_tail, across, table), "gy", other_chip)

    head = jnp.stack((own_head, partner[:HEAD], across, corner))
    to_up, to_down, to_far, own = first_parts(head, down_weight, table)
    table = after(table, own)
    arrived = [
        lax.ppermute(to_up, "gz", z_up),
        lax.ppermute(to_down, "gz", z_down),
        lax.ppermute(to_far, "gz", z_far),
    ]

    near_side = near_terms(preact, grad_output, partner, table, C_SIDE)
    table = after(table, near_side)
    across_tail = after(across_tail, table)
    corner_tail = [
        lax.ppermute(across_tail[start : start + PIECE], "gy", other_core)
        for start in range(0, across_tail.shape[0], PIECE)
    ]
    rows = jnp.stack(
        (
            grad_output,
            partner,
            lax.optimization_barrier(jnp.concatenate((across, across_tail))),
            lax.optimization_barrier(jnp.concatenate((corner, *corner_tail))),
        )
    )

    c_far, d_far = terms(preact, rows, table, C_FAR, near_far)
    table = after(table, c_far)
    c_far = lax.ppermute(c_far, "gx", y_down)
    d_far = lax.ppermute(d_far, "gx", y_up)

    a_far, b_far, a_side, b_side, a_sum, b_sum, own_tail = tail_parts(rows, down_weight, table)
    table = after(table, own_tail)
    a_far = lax.ppermute(after(a_far, *arrived), "gz", z_down)
    b_far = lax.ppermute(after(b_far, *arrived), "gz", z_up)
    table = after(table, *arrived)

    c_side, d_side = terms(preact, rows, table, C_SIDE, near_side)
    table = after(table, c_side)
    c_side = lax.ppermute(after(c_side, c_far, d_far), "gx", y_up)
    d_side = lax.ppermute(after(d_side, c_far, d_far), "gx", y_down)

    table = after(table, c_far, d_far)
    c_sum, d_sum = terms(preact, rows, table, C_SUM, cost=MID)
    table = after(table, c_sum)
    a_side = lax.ppermute(after(a_side, table, a_far, b_far), "gz", z_up)
    b_side = lax.ppermute(after(b_side, table, a_far, b_far), "gz", z_down)
    a_sum = add(a_sum, after(a_far, table)).astype(bf16)
    b_sum = add(b_sum, after(b_far, table)).astype(bf16)
    table = after(table, a_sum, b_sum)

    c_own, d_own = terms(preact, rows, table, C_OWN, cost=LAST)
    table = after(table, c_own)

    c_sum = add(c_sum, c_far).astype(bf16)
    d_sum = add(d_sum, d_far).astype(bf16)
    c_sum = lax.ppermute(after(c_sum, table, c_side, d_side), "gx", y_down)
    d_sum = lax.ppermute(after(d_sum, table, c_side, d_side), "gx", y_up)

    held = head_last(own, arrived, preact, table)
    table = after(table, held)

    a_sum = lax.ppermute(after(a_sum, table, a_side, b_side), "gz", z_down)
    b_sum = lax.ppermute(after(b_sum, table, a_side, b_side), "gz", z_up)

    c_sum, d_sum = after(c_sum, table, a_side, b_side), after(d_sum, table, a_side, b_side)
    c_own = add(c_own, c_side, c_sum)
    d_own = add(d_own, d_side, d_sum)
    keep = jnp.where(h == 0, c_own, d_own)
    give = jnp.where(h == 0, d_own, c_own).astype(bf16)
    taken = lax.ppermute(give, "gx", gx_move(1, 0))
    taken = after(taken, a_sum, b_sum)

    grad_pre = tail_last(own_tail, a_side, a_sum, b_side, b_sum, preact, table, held)
    grad_down = add(keep, taken).astype(bf16)
    return (grad_pre, grad_down)


def solution(mesh):
    return jax.shard_map(
        shards,
        mesh=mesh,
        in_specs=(P("gx", "gy"), P(("gx", "gy"), "gz"), P("gy", "gz")),
        out_specs=(P(("gx", "gz"), "gy"), P(("gy", "gx"), "gz")),
        check_vma=False,
    )
```

```python
import functools
import math

import jax
import jax.numpy as jnp
from jax import lax
from jax.experimental import pallas as pl
from jax.experimental.pallas import tpu as pltpu
from jax.sharding import PartitionSpec as P

root_half = 1.0 / math.sqrt(2.0)
slope_scale = 1.0 / math.sqrt(2.0 * math.pi)
bf16 = jnp.bfloat16
f32 = jnp.float32
HEAD = 160
TILE = 512
PIECE = 96
SHORT, MID, LAST, LONG = 1 / 64, 1/64, 1/64, 1/64
VMEM = 63 * 1024 * 1024


def gelu(values):
    return 0.5 * values * (1.0 + lax.erf(values * root_half))


def unit_slope(values):
    return (
        0.5 * (1.0 + lax.erf(values * root_half))
        + values * jnp.exp(-0.5 * values * values) * slope_scale
    )


def gz_ring(step):
    return [(i, (i + step) % 4) for i in range(4)]


def gx_move(dh, dy):
    return [(h * 4 + y, (h + dh) % 2 * 4 + (y + dy) % 4) for h in range(2) for y in range(4)]


def gy_move(dl, dc):
    return [(l * 2 + c, (l + dl) % 2 * 2 + (c + dc) % 2) for l in range(2) for c in range(2)]


def after(value, *others):
    return lax.optimization_barrier((value,) + others)[0]


def call(body, name, grid, prefetch, in_specs, out_specs, out_shape, flops, moved, scratch=(), cost=1, aliases=None):
    return pl.pallas_call(
        body,
        name=name,
        out_shape=out_shape,
        grid_spec=pltpu.PrefetchScalarGridSpec(
            num_scalar_prefetch=prefetch, grid=grid, in_specs=in_specs, out_specs=out_specs,
            scratch_shapes=list(scratch),
        ),
        compiler_params=pltpu.CompilerParams(
            dimension_semantics=("arbitrary",) * len(grid), vmem_limit_bytes=VMEM
        ),
        input_output_aliases=aliases or {},
        cost_estimate=pl.CostEstimate(
            flops=int(flops * cost), bytes_accessed=int(moved * cost), transcendentals=0
        ),
    )


def rows_dot(rows, weights):
    return lax.dot_general(rows, weights, (((1,), (1,)), ((), ())), preferred_element_type=f32)


def cols_dot(left, right):
    return lax.dot_general(left, right, (((0,), (0,)), ((), ())), preferred_element_type=f32)


ORDER, FAR, UP, DOWN, OWN, GZ = 0, 4, 5, 6, 7, 8
C_FAR, C_SIDE, C_SUM, C_OWN = 10, 12, 14, 16


def first_body(table, rows, weights, up, down, far, own, part):
    count = up.shape[0]
    total = rows_dot(rows[...], weights[...]).astype(bf16)
    for j in range(4):
        part[j] = total[j * count : (j + 1) * count]
    up[...] = part[table[UP]]
    down[...] = part[table[DOWN]]
    far[...] = part[table[FAR]]
    own[...] = part[table[OWN]]


def first_parts(rows, weights, table):
    _, count, depth = rows.shape
    hidden = weights.shape[0]
    block = pl.BlockSpec((count, TILE), lambda t, o: (0, t))
    return call(
        first_body,
        "first_parts",
        (hidden // TILE,),
        1,
        [
            pl.BlockSpec((4 * count, depth), lambda t, o: (0, 0)),
            pl.BlockSpec((TILE, depth), lambda t, o: (t, 0)),
        ],
        [block] * 4,
        [jax.ShapeDtypeStruct((count, hidden), bf16)] * 4,
        8 * count * depth * hidden,
        2 * (4 * count * depth + depth * hidden + 4 * count * hidden),
        scratch=[pltpu.VMEM((4, count, TILE), bf16)],
        cost=SHORT,
    )(table, rows.reshape(4 * count, depth), weights)


def tail_body(table, rows, weights, far_a, far_b, side_a, side_b, sum_a, sum_b, own, left, part):
    count = own.shape[0]
    first = pl.program_id(0) < pl.num_programs(0) // 2

    @pl.when(pl.program_id(0) == 0)
    def _():
        for j in range(4):
            left[j * count : (j + 1) * count] = rows[j, HEAD:]

    total = rows_dot(left[...], weights[...]).astype(bf16)
    for j in range(4):
        part[j] = total[j * count : (j + 1) * count]
    own[...] = part[table[OWN]]

    @pl.when(first)
    def _():
        far_a[...] = part[table[FAR]]
        side_a[...] = part[table[UP]]
        sum_a[...] = part[table[DOWN]]

    @pl.when(jnp.logical_not(first))
    def _():
        far_b[...] = part[table[FAR]]
        side_b[...] = part[table[DOWN]]
        sum_b[...] = part[table[UP]]


def tail_parts(rows, weights, table):
    _, share, depth = rows.shape
    count = share - HEAD
    hidden = weights.shape[0]
    tiles = hidden // TILE
    half_a = pl.BlockSpec((count, TILE), lambda t, p: (0, jnp.minimum(t, tiles // 2 - 1)))
    half_b = pl.BlockSpec((count, TILE), lambda t, p: (0, jnp.maximum(t - tiles // 2, 0)))
    half = jax.ShapeDtypeStruct((count, hidden // 2), bf16)
    return call(
        tail_body,
        "tail_parts",
        (tiles,),
        1,
        [
            pl.BlockSpec((4, share, depth), lambda t, o: (0, 0, 0)),
            pl.BlockSpec((TILE, depth), lambda t, o: (t, 0)),
        ],
        [half_a, half_b] * 3 + [pl.BlockSpec((count, TILE), lambda t, o: (0, t))],
        [half] * 6 + [jax.ShapeDtypeStruct((count, hidden), bf16)],
        8 * count * depth * hidden,
        2 * (4 * share * depth + depth * hidden + 4 * count * hidden),
        scratch=[pltpu.VMEM((4 * count, depth), bf16), pltpu.VMEM((4, count, TILE), bf16)],
        cost=SHORT,
    )(table, rows, weights)


def head_last_body(table, own, one, two, three, pre, out):
    total = own[...].astype(f32) + one[...].astype(f32)
    total += two[...].astype(f32) + three[...].astype(f32)
    out[...] = (total * unit_slope(pre[: own.shape[0]].astype(f32))).astype(bf16)


def head_last(own, arrived, preact, table):
    count, hidden = own.shape
    share = preact.shape[0] // 4
    width = hidden // 2
    block = pl.BlockSpec((count, width), lambda t, p: (0, t))
    return call(
        head_last_body,
        "head_last",
        (2,),
        1,
        [block] * 4
        + [pl.BlockSpec((share, width), lambda t, p: (p[GZ], t))],
        block,
        jax.ShapeDtypeStruct((count, hidden), bf16),
        count * hidden * 40,
        12 * count * hidden,
        cost=LONG,
    )(table, own, *arrived, preact)


def tail_last_body(table, own, side_a, sum_a, side_b, sum_b, pre, held, out):
    head = held.shape[0]
    slope = unit_slope(pre[head:].astype(f32))
    total = own[...].astype(f32)
    first = pl.program_id(0) < pl.num_programs(0) // 2
    out[:head] = held[...]

    @pl.when(first)
    def _():
        whole = total + side_a[...].astype(f32) + sum_a[...].astype(f32)
        out[head:] = (whole * slope).astype(bf16)

    @pl.when(jnp.logical_not(first))
    def _():
        whole = total + side_b[...].astype(f32) + sum_b[...].astype(f32)
        out[head:] = (whole * slope).astype(bf16)


def tail_last(own, side_a, sum_a, side_b, sum_b, preact, table, held):
    count, hidden = own.shape
    share = preact.shape[0] // 4
    tiles = hidden // TILE
    half_a = pl.BlockSpec((count, TILE), lambda t, p: (0, jnp.minimum(t, tiles // 2 - 1)))
    half_b = pl.BlockSpec((count, TILE), lambda t, p: (0, jnp.maximum(t - tiles // 2, 0)))
    return call(
        tail_last_body,
        "tail_last",
        (tiles,),
        1,
        [
            pl.BlockSpec((count, TILE), lambda t, p: (0, t)),
            half_a,
            half_a,
            half_b,
            half_b,
            pl.BlockSpec((share, TILE), lambda t, p: (p[GZ], t)),
            pl.BlockSpec((share - count, TILE), lambda t, p: (0, t)),
        ],
        pl.BlockSpec((share, TILE), lambda t, p: (0, t)),
        jax.ShapeDtypeStruct((share, hidden), bf16),
        count * hidden * 40,
        10 * count * hidden,
    )(table, own, side_a, sum_a, side_b, sum_b, preact, held)


def near_body(table, pre_own, pre_partner, own, partner, out):
    total = cols_dot(gelu(pre_own[...].astype(f32)).astype(bf16), own[...])
    total += cols_dot(gelu(pre_partner[...].astype(f32)).astype(bf16), partner[...])
    out[0] = total.astype(bf16)


def near_terms(preact, own, partner, table, at, cost=SHORT):
    rows, hidden = preact.shape
    share, features = own.shape
    chunk = hidden // 8
    return call(
        near_body,
        "near_terms",
        (2,),
        1,
        [
            pl.BlockSpec((share, chunk), lambda t, p: (p[ORDER], p[at + t])),
            pl.BlockSpec((share, chunk), lambda t, p: (p[ORDER + 1], p[at + t])),
            pl.BlockSpec((share, features), lambda t, p: (0, 0)),
            pl.BlockSpec((share, features), lambda t, p: (0, 0)),
        ],
        pl.BlockSpec((1, chunk, features), lambda t, p: (t, 0, 0)),
        jax.ShapeDtypeStruct((2, chunk, features), bf16),
        8 * share * features * chunk,
        2 * (4 * share * chunk + 2 * share * features + 2 * features * chunk),
        cost=cost,
    )(table, preact, preact, own, partner)


def terms_body(near, table, *refs):
    extra = refs[-4] if near else None
    rows, out_a, out_b = refs[-3:]
    total = None
    share = refs[0].shape[0]
    for j, pre in enumerate(refs[: 2 if near else 4]):
        act = gelu(pre[...].astype(f32)).astype(bf16)
        term = cols_dot(act, rows[j])
        total = term if total is None else total + term
    if near:
        total += extra[0].astype(f32)

    @pl.when(pl.program_id(0) == 0)
    def _():
        out_a[...] = total.astype(bf16)

    @pl.when(pl.program_id(0) == 1)
    def _():
        out_b[...] = total.astype(bf16)


def terms(preact, rows, table, at, held=None, cost=SHORT):
    hidden = preact.shape[1]
    _, share, features = rows.shape
    chunk = hidden // 8
    near = held is not None
    pieces = (2, 3) if near else (0, 1, 2, 3)

    def source(j):
        return pl.BlockSpec((share, chunk), lambda t, p: (p[ORDER + j], p[at + t]))

    out = pl.BlockSpec((chunk, features), lambda t, p: (0, 0))
    return call(
        functools.partial(terms_body, near),
        "terms",
        (2,),
        1,
        [source(j) for j in pieces]
        + [pl.BlockSpec((1, chunk, features), lambda t, p: (t, 0, 0))] * near
        + [pl.BlockSpec((len(pieces), share, features), lambda t, p: (int(near), 0, 0))],
        [out, out],
        [jax.ShapeDtypeStruct((chunk, features), bf16)] * 2,
        4 * len(pieces) * share * features * chunk,
        2 * (2 * len(pieces) * share * chunk + len(pieces) * share * features),
        cost=cost,
    )(table, *[preact] * len(pieces), *([held] if near else []), rows)


def shards(preact, grad_output, down_weight):
    gy = lax.axis_index("gy")
    gz = lax.axis_index("gz")
    gx = lax.axis_index("gx")
    y, h = gx % 4, gx // 4
    entries = [gy ^ j for j in range(4)]
    entries += [(gz + 2) % 4 ^ gy, (gz + 1) % 4 ^ gy, (gz + 3) % 4 ^ gy, gz ^ gy, gz, 0]
    up, down, far = (y + 1) % 4, (y + 3) % 4, (y + 2) % 4
    entries += [far, 4 + far, up, 4 + down, down, 4 + up, y, 4 + y]
    table = jnp.stack([jnp.asarray(entry, jnp.int32) for entry in entries])

    other_chip, other_core = gy_move(1, 0), gy_move(0, 1)
    z_up, z_down, z_far = gz_ring(1), gz_ring(-1), gz_ring(2)
    y_up, y_down = gx_move(0, 1), gx_move(0, -1)

    def add(*values):
        return sum(value.astype(f32) for value in values)

    own_head, own_tail = grad_output[:HEAD], grad_output[HEAD:]
    across = lax.ppermute(own_head, "gy", other_chip)
    partner = lax.ppermute(grad_output, "gy", other_core)
    near_far = near_terms(preact, grad_output, partner, table, C_FAR)
    table = after(table, near_far)
    corner = lax.ppermute(after(across, table), "gy", other_core)
    across_tail = lax.ppermute(after(own_tail, across, table), "gy", other_chip)

    head = jnp.stack((own_head, partner[:HEAD], across, corner))
    to_up, to_down, to_far, own = first_parts(head, down_weight, table)
    table = after(table, own)
    arrived = [
        lax.ppermute(to_up, "gz", z_up),
        lax.ppermute(to_down, "gz", z_down),
        lax.ppermute(to_far, "gz", z_far),
    ]

    near_side = near_terms(preact, grad_output, partner, table, C_SIDE)
    table = after(table, near_side)
    across_tail = after(across_tail, table)
    corner_tail = [
        lax.ppermute(across_tail[start : start + PIECE], "gy", other_core)
        for start in range(0, across_tail.shape[0], PIECE)
    ]
    rows = jnp.stack(
        (
            grad_output,
            partner,
            lax.optimization_barrier(jnp.concatenate((across, across_tail))),
            lax.optimization_barrier(jnp.concatenate((corner, *corner_tail))),
        )
    )

    c_far, d_far = terms(preact, rows, table, C_FAR, near_far)
    table = after(table, c_far)
    c_far = lax.ppermute(c_far, "gx", y_down)
    d_far = lax.ppermute(d_far, "gx", y_up)

    a_far, b_far, a_side, b_side, a_sum, b_sum, own_tail = tail_parts(rows, down_weight, table)
    table = after(table, own_tail)
    a_far = lax.ppermute(after(a_far, *arrived), "gz", z_down)
    b_far = lax.ppermute(after(b_far, *arrived), "gz", z_up)
    table = after(table, *arrived)

    c_side, d_side = terms(preact, rows, table, C_SIDE, near_side)
    table = after(table, c_side)
    c_side = lax.ppermute(after(c_side, c_far, d_far), "gx", y_up)
    d_side = lax.ppermute(after(d_side, c_far, d_far), "gx", y_down)

    table = after(table, c_far, d_far)
    c_sum, d_sum = terms(preact, rows, table, C_SUM, cost=MID)
    table = after(table, c_sum)
    a_side = lax.ppermute(after(a_side, table, a_far, b_far), "gz", z_up)
    b_side = lax.ppermute(after(b_side, table, a_far, b_far), "gz", z_down)
    a_sum = add(a_sum, after(a_far, table)).astype(bf16)
    b_sum = add(b_sum, after(b_far, table)).astype(bf16)
    c_sum = add(c_sum, c_far).astype(bf16)
    d_sum = add(d_sum, d_far).astype(bf16)
    table = after(table, a_sum, b_sum, c_sum)

    c_sum = lax.ppermute(after(c_sum, c_side, d_side), "gx", y_down)
    d_sum = lax.ppermute(after(d_sum, c_side, d_side), "gx", y_up)
    table = after(table, c_side, d_side)

    c_own, d_own = terms(preact, rows, table, C_OWN, cost=LAST)
    table = after(table, c_own)

    held = head_last(own, arrived, preact, table)
    table = after(table, held)

    a_sum = lax.ppermute(after(a_sum, table, a_side, b_side), "gz", z_down)
    b_sum = lax.ppermute(after(b_sum, table, a_side, b_side), "gz", z_up)

    c_sum, d_sum = after(c_sum, table, a_side, b_side), after(d_sum, table, a_side, b_side)
    c_own = add(c_own, c_side, c_sum)
    d_own = add(d_own, d_side, d_sum)
    keep = jnp.where(h == 0, c_own, d_own)
    give = jnp.where(h == 0, d_own, c_own).astype(bf16)
    taken = lax.ppermute(give, "gx", gx_move(1, 0))
    taken = after(taken, a_sum, b_sum)

    grad_pre = tail_last(own_tail, a_side, a_sum, b_side, b_sum, preact, table, held)
    grad_down = add(keep, taken).astype(bf16)
    return (grad_pre, grad_down)


def solution(mesh):
    return jax.shard_map(
        shards,
        mesh=mesh,
        in_specs=(P("gx", "gy"), P(("gx", "gy"), "gz"), P("gy", "gz")),
        out_specs=(P(("gx", "gz"), "gy"), P(("gy", "gx"), "gz")),
        check_vma=False,
    )
```

```python
import functools
import math

import jax
import jax.numpy as jnp
from jax import lax
from jax.experimental import pallas as pl
from jax.experimental.pallas import tpu as pltpu
from jax.sharding import PartitionSpec as P

root_half = 1.0 / math.sqrt(2.0)
slope_scale = 1.0 / math.sqrt(2.0 * math.pi)
bf16 = jnp.bfloat16
f32 = jnp.float32
HEAD = 160
TILE = 512
PIECE = 96
SHORT, MID, LAST, LONG = 1 / 64, 1/64, 1/64, 1/64
VMEM = 63 * 1024 * 1024


def gelu(values):
    return 0.5 * values * (1.0 + lax.erf(values * root_half))


def unit_slope(values):
    return (
        0.5 * (1.0 + lax.erf(values * root_half))
        + values * jnp.exp(-0.5 * values * values) * slope_scale
    )


def gz_ring(step):
    return [(i, (i + step) % 4) for i in range(4)]


def gx_move(dh, dy):
    return [(h * 4 + y, (h + dh) % 2 * 4 + (y + dy) % 4) for h in range(2) for y in range(4)]


def gy_move(dl, dc):
    return [(l * 2 + c, (l + dl) % 2 * 2 + (c + dc) % 2) for l in range(2) for c in range(2)]


def after(value, *others):
    return lax.optimization_barrier((value,) + others)[0]


def call(body, name, grid, prefetch, in_specs, out_specs, out_shape, flops, moved, scratch=(), cost=1, aliases=None):
    return pl.pallas_call(
        body,
        name=name,
        out_shape=out_shape,
        grid_spec=pltpu.PrefetchScalarGridSpec(
            num_scalar_prefetch=prefetch, grid=grid, in_specs=in_specs, out_specs=out_specs,
            scratch_shapes=list(scratch),
        ),
        compiler_params=pltpu.CompilerParams(
            dimension_semantics=("arbitrary",) * len(grid), vmem_limit_bytes=VMEM
        ),
        input_output_aliases=aliases or {},
        cost_estimate=pl.CostEstimate(
            flops=int(flops * cost), bytes_accessed=int(moved * cost), transcendentals=0
        ),
    )


def rows_dot(rows, weights):
    return lax.dot_general(rows, weights, (((1,), (1,)), ((), ())), preferred_element_type=f32)


def cols_dot(left, right):
    return lax.dot_general(left, right, (((0,), (0,)), ((), ())), preferred_element_type=f32)


ORDER, FAR, UP, DOWN, OWN, GZ = 0, 4, 5, 6, 7, 8
C_FAR, C_SIDE, C_SUM, C_OWN = 10, 12, 14, 16


def first_body(table, rows, weights, up, down, far, own, part):
    count = up.shape[0]
    total = rows_dot(rows[...], weights[...]).astype(bf16)
    for j in range(4):
        part[j] = total[j * count : (j + 1) * count]
    up[...] = part[table[UP]]
    down[...] = part[table[DOWN]]
    far[...] = part[table[FAR]]
    own[...] = part[table[OWN]]


def first_parts(rows, weights, table):
    _, count, depth = rows.shape
    hidden = weights.shape[0]
    block = pl.BlockSpec((count, TILE), lambda t, o: (0, t))
    return call(
        first_body,
        "first_parts",
        (hidden // TILE,),
        1,
        [
            pl.BlockSpec((4 * count, depth), lambda t, o: (0, 0)),
            pl.BlockSpec((TILE, depth), lambda t, o: (t, 0)),
        ],
        [block] * 4,
        [jax.ShapeDtypeStruct((count, hidden), bf16)] * 4,
        8 * count * depth * hidden,
        2 * (4 * count * depth + depth * hidden + 4 * count * hidden),
        scratch=[pltpu.VMEM((4, count, TILE), bf16)],
        cost=SHORT,
    )(table, rows.reshape(4 * count, depth), weights)


def tail_body(table, rows, weights, far_a, far_b, side_a, side_b, sum_a, sum_b, own, left, part):
    count = own.shape[0]
    first = pl.program_id(0) < pl.num_programs(0) // 2

    @pl.when(pl.program_id(0) == 0)
    def _():
        for j in range(4):
            left[j * count : (j + 1) * count] = rows[j, HEAD:]

    total = rows_dot(left[...], weights[...]).astype(bf16)
    for j in range(4):
        part[j] = total[j * count : (j + 1) * count]
    own[...] = part[table[OWN]]

    @pl.when(first)
    def _():
        far_a[...] = part[table[FAR]]
        side_a[...] = part[table[UP]]
        sum_a[...] = part[table[DOWN]]

    @pl.when(jnp.logical_not(first))
    def _():
        far_b[...] = part[table[FAR]]
        side_b[...] = part[table[DOWN]]
        sum_b[...] = part[table[UP]]


def tail_parts(rows, weights, table):
    _, share, depth = rows.shape
    count = share - HEAD
    hidden = weights.shape[0]
    tiles = hidden // TILE
    half_a = pl.BlockSpec((count, TILE), lambda t, p: (0, jnp.minimum(t, tiles // 2 - 1)))
    half_b = pl.BlockSpec((count, TILE), lambda t, p: (0, jnp.maximum(t - tiles // 2, 0)))
    half = jax.ShapeDtypeStruct((count, hidden // 2), bf16)
    return call(
        tail_body,
        "tail_parts",
        (tiles,),
        1,
        [
            pl.BlockSpec((4, share, depth), lambda t, o: (0, 0, 0)),
            pl.BlockSpec((TILE, depth), lambda t, o: (t, 0)),
        ],
        [half_a, half_b] * 3 + [pl.BlockSpec((count, TILE), lambda t, o: (0, t))],
        [half] * 6 + [jax.ShapeDtypeStruct((count, hidden), bf16)],
        8 * count * depth * hidden,
        2 * (4 * share * depth + depth * hidden + 4 * count * hidden),
        scratch=[pltpu.VMEM((4 * count, depth), bf16), pltpu.VMEM((4, count, TILE), bf16)],
        cost=SHORT,
    )(table, rows, weights)


def head_last_body(table, own, one, two, three, pre, out):
    total = own[...].astype(f32) + one[...].astype(f32)
    total += two[...].astype(f32) + three[...].astype(f32)
    out[...] = (total * unit_slope(pre[: own.shape[0]].astype(f32))).astype(bf16)


def head_last(own, arrived, preact, table):
    count, hidden = own.shape
    share = preact.shape[0] // 4
    width = hidden // 2
    block = pl.BlockSpec((count, width), lambda t, p: (0, t))
    return call(
        head_last_body,
        "head_last",
        (2,),
        1,
        [block] * 4
        + [pl.BlockSpec((share, width), lambda t, p: (p[GZ], t))],
        block,
        jax.ShapeDtypeStruct((count, hidden), bf16),
        count * hidden * 40,
        12 * count * hidden,
        cost=LONG,
    )(table, own, *arrived, preact)


def ready_body(table, own, side_a, side_b, pre, held, partial, slope):
    head = held.shape[0]
    slope[...] = unit_slope(pre[head:].astype(f32)).astype(bf16)
    total = own[...].astype(f32)
    first = pl.program_id(0) < pl.num_programs(0) // 2
    partial[:head] = held[...]

    @pl.when(first)
    def _():
        partial[head:] = (total + side_a[...].astype(f32)).astype(bf16)

    @pl.when(jnp.logical_not(first))
    def _():
        partial[head:] = (total + side_b[...].astype(f32)).astype(bf16)


def halves(count, hidden):
    tiles = hidden // TILE
    return [
        pl.BlockSpec((count, TILE), lambda t, p: (0, jnp.minimum(t, tiles // 2 - 1))),
        pl.BlockSpec((count, TILE), lambda t, p: (0, jnp.maximum(t - tiles // 2, 0))),
    ]


def tail_ready(own, side_a, side_b, preact, table, held):
    count, hidden = own.shape
    share = preact.shape[0] // 4
    block = pl.BlockSpec((count, TILE), lambda t, p: (0, t))
    return call(
        ready_body,
        "tail_ready",
        (hidden // TILE,),
        1,
        [block]
        + halves(count, hidden)
        + [
            pl.BlockSpec((share, TILE), lambda t, p: (p[GZ], t)),
            pl.BlockSpec((share - count, TILE), lambda t, p: (0, t)),
        ],
        [pl.BlockSpec((share, TILE), lambda t, p: (0, t)), block],
        [jax.ShapeDtypeStruct((share, hidden), bf16), jax.ShapeDtypeStruct((count, hidden), bf16)],
        count * hidden * 40,
        10 * count * hidden,
        cost=SHORT,
    )(table, own, side_a, side_b, preact, held)


def tail_last_body(table, partial, slope, sum_a, sum_b, keep, taken, out, down):
    head = out.shape[0] - slope.shape[0]
    out[:head] = partial[:head]
    down[...] = (keep[...] + taken[...].astype(f32)).astype(bf16)
    total = partial[head:].astype(f32)
    first = pl.program_id(0) < pl.num_programs(0) // 2

    @pl.when(first)
    def _():
        out[head:] = ((total + sum_a[...].astype(f32)) * slope[...].astype(f32)).astype(bf16)

    @pl.when(jnp.logical_not(first))
    def _():
        out[head:] = ((total + sum_b[...].astype(f32)) * slope[...].astype(f32)).astype(bf16)


def tail_last(partial, slope, sum_a, sum_b, keep, taken, table):
    count, hidden = slope.shape
    share = partial.shape[0]
    chunk, features = keep.shape
    tiles = hidden // TILE
    whole = pl.BlockSpec((share, TILE), lambda t, p: (0, t))
    down = pl.BlockSpec((chunk // tiles, features), lambda t, p: (t, 0))
    return call(
        tail_last_body,
        "tail_last",
        (tiles,),
        1,
        [whole, pl.BlockSpec((count, TILE), lambda t, p: (0, t))]
        + halves(count, hidden)
        + [down, down],
        [whole, down],
        [
            jax.ShapeDtypeStruct((share, hidden), bf16),
            jax.ShapeDtypeStruct((chunk, features), bf16),
        ],
        count * hidden * 4,
        10 * count * hidden,
    )(table, partial, slope, sum_a, sum_b, keep, taken)


def near_body(table, pre_own, pre_partner, own, partner, out):
    total = cols_dot(gelu(pre_own[...].astype(f32)).astype(bf16), own[...])
    total += cols_dot(gelu(pre_partner[...].astype(f32)).astype(bf16), partner[...])
    out[0] = total.astype(bf16)


def near_terms(preact, own, partner, table, at, cost=SHORT):
    rows, hidden = preact.shape
    share, features = own.shape
    chunk = hidden // 8
    return call(
        near_body,
        "near_terms",
        (2,),
        1,
        [
            pl.BlockSpec((share, chunk), lambda t, p: (p[ORDER], p[at + t])),
            pl.BlockSpec((share, chunk), lambda t, p: (p[ORDER + 1], p[at + t])),
            pl.BlockSpec((share, features), lambda t, p: (0, 0)),
            pl.BlockSpec((share, features), lambda t, p: (0, 0)),
        ],
        pl.BlockSpec((1, chunk, features), lambda t, p: (t, 0, 0)),
        jax.ShapeDtypeStruct((2, chunk, features), bf16),
        8 * share * features * chunk,
        2 * (4 * share * chunk + 2 * share * features + 2 * features * chunk),
        cost=cost,
    )(table, preact, preact, own, partner)


def terms_body(near, table, *refs):
    extra = refs[-4] if near else None
    rows, out_a, out_b = refs[-3:]
    total = None
    share = refs[0].shape[0]
    for j, pre in enumerate(refs[: 2 if near else 4]):
        act = gelu(pre[...].astype(f32)).astype(bf16)
        term = cols_dot(act, rows[j])
        total = term if total is None else total + term
    if near:
        total += extra[0].astype(f32)

    @pl.when(pl.program_id(0) == 0)
    def _():
        out_a[...] = total.astype(bf16)

    @pl.when(pl.program_id(0) == 1)
    def _():
        out_b[...] = total.astype(bf16)


def terms(preact, rows, table, at, held=None, cost=SHORT):
    hidden = preact.shape[1]
    _, share, features = rows.shape
    chunk = hidden // 8
    near = held is not None
    pieces = (2, 3) if near else (0, 1, 2, 3)

    def source(j):
        return pl.BlockSpec((share, chunk), lambda t, p: (p[ORDER + j], p[at + t]))

    out = pl.BlockSpec((chunk, features), lambda t, p: (0, 0))
    return call(
        functools.partial(terms_body, near),
        "terms",
        (2,),
        1,
        [source(j) for j in pieces]
        + [pl.BlockSpec((1, chunk, features), lambda t, p: (t, 0, 0))] * near
        + [pl.BlockSpec((len(pieces), share, features), lambda t, p: (int(near), 0, 0))],
        [out, out],
        [jax.ShapeDtypeStruct((chunk, features), bf16)] * 2,
        4 * len(pieces) * share * features * chunk,
        2 * (2 * len(pieces) * share * chunk + len(pieces) * share * features),
        cost=cost,
    )(table, *[preact] * len(pieces), *([held] if near else []), rows)


def shards(preact, grad_output, down_weight):
    gy = lax.axis_index("gy")
    gz = lax.axis_index("gz")
    gx = lax.axis_index("gx")
    y, h = gx % 4, gx // 4
    entries = [gy ^ j for j in range(4)]
    entries += [(gz + 2) % 4 ^ gy, (gz + 1) % 4 ^ gy, (gz + 3) % 4 ^ gy, gz ^ gy, gz, 0]
    up, down, far = (y + 1) % 4, (y + 3) % 4, (y + 2) % 4
    entries += [far, 4 + far, up, 4 + down, down, 4 + up, y, 4 + y]
    table = jnp.stack([jnp.asarray(entry, jnp.int32) for entry in entries])

    other_chip, other_core = gy_move(1, 0), gy_move(0, 1)
    z_up, z_down, z_far = gz_ring(1), gz_ring(-1), gz_ring(2)
    y_up, y_down = gx_move(0, 1), gx_move(0, -1)

    def add(*values):
        return sum(value.astype(f32) for value in values)

    own_head, own_tail = grad_output[:HEAD], grad_output[HEAD:]
    across = lax.ppermute(own_head, "gy", other_chip)
    partner = lax.ppermute(grad_output, "gy", other_core)
    near_far = near_terms(preact, grad_output, partner, table, C_FAR)
    table = after(table, near_far)
    corner = lax.ppermute(after(across, table), "gy", other_core)
    across_tail = lax.ppermute(after(own_tail, across, table), "gy", other_chip)

    head = jnp.stack((own_head, partner[:HEAD], across, corner))
    to_up, to_down, to_far, own = first_parts(head, down_weight, table)
    table = after(table, own)
    arrived = [
        lax.ppermute(to_up, "gz", z_up),
        lax.ppermute(to_down, "gz", z_down),
        lax.ppermute(to_far, "gz", z_far),
    ]

    near_side = near_terms(preact, grad_output, partner, table, C_SIDE)
    table = after(table, near_side)
    across_tail = after(across_tail, table)
    corner_tail = [
        lax.ppermute(across_tail[start : start + PIECE], "gy", other_core)
        for start in range(0, across_tail.shape[0], PIECE)
    ]
    rows = jnp.stack(
        (
            grad_output,
            partner,
            lax.optimization_barrier(jnp.concatenate((across, across_tail))),
            lax.optimization_barrier(jnp.concatenate((corner, *corner_tail))),
        )
    )

    c_far, d_far = terms(preact, rows, table, C_FAR, near_far)
    table = after(table, c_far)
    c_far = lax.ppermute(c_far, "gx", y_down)
    d_far = lax.ppermute(d_far, "gx", y_up)

    a_far, b_far, a_side, b_side, a_sum, b_sum, own_tail = tail_parts(rows, down_weight, table)
    table = after(table, own_tail)
    a_far = lax.ppermute(after(a_far, *arrived), "gz", z_down)
    b_far = lax.ppermute(after(b_far, *arrived), "gz", z_up)
    table = after(table, *arrived)

    c_side, d_side = terms(preact, rows, table, C_SIDE, near_side)
    table = after(table, c_side)
    c_side = lax.ppermute(after(c_side, c_far, d_far), "gx", y_up)
    d_side = lax.ppermute(after(d_side, c_far, d_far), "gx", y_down)

    table = after(table, c_far, d_far)
    c_sum, d_sum = terms(preact, rows, table, C_SUM, cost=MID)
    table = after(table, c_sum)
    a_side = lax.ppermute(after(a_side, table, a_far, b_far), "gz", z_up)
    b_side = lax.ppermute(after(b_side, table, a_far, b_far), "gz", z_down)
    a_sum = add(a_sum, after(a_far, table)).astype(bf16)
    b_sum = add(b_sum, after(b_far, table)).astype(bf16)
    c_sum = add(c_sum, c_far).astype(bf16)
    d_sum = add(d_sum, d_far).astype(bf16)
    table = after(table, a_sum, b_sum, c_sum)

    c_sum = lax.ppermute(after(c_sum, c_side, d_side), "gx", y_down)
    d_sum = lax.ppermute(after(d_sum, c_side, d_side), "gx", y_up)
    table = after(table, c_side, d_side)

    c_own, d_own = terms(preact, rows, table, C_OWN, cost=LAST)
    table = after(table, c_own)

    held = head_last(own, arrived, preact, table)
    table = after(table, held)

    a_sum = lax.ppermute(after(a_sum, table, a_side, b_side), "gz", z_down)
    b_sum = lax.ppermute(after(b_sum, table, a_side, b_side), "gz", z_up)

    c_sum, d_sum = after(c_sum, table, a_side, b_side), after(d_sum, table, a_side, b_side)
    c_own = add(c_own, c_side, c_sum)
    d_own = add(d_own, d_side, d_sum)
    keep = jnp.where(h == 0, c_own, d_own)
    give = jnp.where(h == 0, d_own, c_own).astype(bf16)
    taken = lax.ppermute(give, "gx", gx_move(1, 0))
    own_tail = after(own_tail, give)
    partial, slope = tail_ready(own_tail, a_side, b_side, preact, table, held)
    grad_pre, grad_down = tail_last(partial, slope, a_sum, b_sum, keep, taken, table)
    return (grad_pre, grad_down)


def solution(mesh):
    return jax.shard_map(
        shards,
        mesh=mesh,
        in_specs=(P("gx", "gy"), P(("gx", "gy"), "gz"), P("gy", "gz")),
        out_specs=(P(("gx", "gz"), "gy"), P(("gy", "gx"), "gz")),
        check_vma=False,
    )
```

```python
import functools
import math

import jax
import jax.numpy as jnp
from jax import lax
from jax.experimental import pallas as pl
from jax.experimental.pallas import tpu as pltpu
from jax.sharding import PartitionSpec as P

root_half = 1.0 / math.sqrt(2.0)
slope_scale = 1.0 / math.sqrt(2.0 * math.pi)
bf16 = jnp.bfloat16
f32 = jnp.float32
HEAD = 160
TILE = 512
PIECE = 96
SHORT, MID, LAST, LONG = 1 / 64, 1/64, 1/64, 1/64
VMEM = 63 * 1024 * 1024


def gelu(values):
    return 0.5 * values * (1.0 + lax.erf(values * root_half))


def unit_slope(values):
    return (
        0.5 * (1.0 + lax.erf(values * root_half))
        + values * jnp.exp(-0.5 * values * values) * slope_scale
    )


def gz_ring(step):
    return [(i, (i + step) % 4) for i in range(4)]


def gx_move(dh, dy):
    return [(h * 4 + y, (h + dh) % 2 * 4 + (y + dy) % 4) for h in range(2) for y in range(4)]


def gy_move(dl, dc):
    return [(l * 2 + c, (l + dl) % 2 * 2 + (c + dc) % 2) for l in range(2) for c in range(2)]


def after(value, *others):
    return lax.optimization_barrier((value,) + others)[0]


def call(body, name, grid, prefetch, in_specs, out_specs, out_shape, flops, moved, scratch=(), cost=1, aliases=None):
    return pl.pallas_call(
        body,
        name=name,
        out_shape=out_shape,
        grid_spec=pltpu.PrefetchScalarGridSpec(
            num_scalar_prefetch=prefetch, grid=grid, in_specs=in_specs, out_specs=out_specs,
            scratch_shapes=list(scratch),
        ),
        compiler_params=pltpu.CompilerParams(
            dimension_semantics=("arbitrary",) * len(grid), vmem_limit_bytes=VMEM
        ),
        input_output_aliases=aliases or {},
        cost_estimate=pl.CostEstimate(
            flops=int(flops * cost), bytes_accessed=int(moved * cost), transcendentals=0
        ),
    )


def rows_dot(rows, weights):
    return lax.dot_general(rows, weights, (((1,), (1,)), ((), ())), preferred_element_type=f32)


def cols_dot(left, right):
    return lax.dot_general(left, right, (((0,), (0,)), ((), ())), preferred_element_type=f32)


ORDER, FAR, UP, DOWN, OWN, GZ = 0, 4, 5, 6, 7, 8
C_FAR, C_SIDE, C_SUM, C_OWN = 10, 12, 14, 16


def first_body(table, rows, weights, up, down, far, own, part):
    count = up.shape[0]
    total = rows_dot(rows[...], weights[...]).astype(bf16)
    for j in range(4):
        part[j] = total[j * count : (j + 1) * count]
    up[...] = part[table[UP]]
    down[...] = part[table[DOWN]]
    far[...] = part[table[FAR]]
    own[...] = part[table[OWN]]


def first_parts(rows, weights, table):
    _, count, depth = rows.shape
    hidden = weights.shape[0]
    block = pl.BlockSpec((count, TILE), lambda t, o: (0, t))
    return call(
        first_body,
        "first_parts",
        (hidden // TILE,),
        1,
        [
            pl.BlockSpec((4 * count, depth), lambda t, o: (0, 0)),
            pl.BlockSpec((TILE, depth), lambda t, o: (t, 0)),
        ],
        [block] * 4,
        [jax.ShapeDtypeStruct((count, hidden), bf16)] * 4,
        8 * count * depth * hidden,
        2 * (4 * count * depth + depth * hidden + 4 * count * hidden),
        scratch=[pltpu.VMEM((4, count, TILE), bf16)],
        cost=SHORT,
    )(table, rows.reshape(4 * count, depth), weights)


def tail_body(table, rows, weights, far_a, far_b, side_a, side_b, sum_a, sum_b, own, left, part):
    count = own.shape[0]
    first = pl.program_id(0) < pl.num_programs(0) // 2

    @pl.when(pl.program_id(0) == 0)
    def _():
        for j in range(4):
            left[j * count : (j + 1) * count] = rows[j, HEAD:]

    total = rows_dot(left[...], weights[...]).astype(bf16)
    for j in range(4):
        part[j] = total[j * count : (j + 1) * count]
    own[...] = part[table[OWN]]

    @pl.when(first)
    def _():
        far_a[...] = part[table[FAR]]
        side_a[...] = part[table[UP]]
        sum_a[...] = part[table[DOWN]]

    @pl.when(jnp.logical_not(first))
    def _():
        far_b[...] = part[table[FAR]]
        side_b[...] = part[table[DOWN]]
        sum_b[...] = part[table[UP]]


def tail_parts(rows, weights, table):
    _, share, depth = rows.shape
    count = share - HEAD
    hidden = weights.shape[0]
    tiles = hidden // TILE
    half_a = pl.BlockSpec((count, TILE), lambda t, p: (0, jnp.minimum(t, tiles // 2 - 1)))
    half_b = pl.BlockSpec((count, TILE), lambda t, p: (0, jnp.maximum(t - tiles // 2, 0)))
    half = jax.ShapeDtypeStruct((count, hidden // 2), bf16)
    return call(
        tail_body,
        "tail_parts",
        (tiles,),
        1,
        [
            pl.BlockSpec((4, share, depth), lambda t, o: (0, 0, 0)),
            pl.BlockSpec((TILE, depth), lambda t, o: (t, 0)),
        ],
        [half_a, half_b] * 3 + [pl.BlockSpec((count, TILE), lambda t, o: (0, t))],
        [half] * 6 + [jax.ShapeDtypeStruct((count, hidden), bf16)],
        8 * count * depth * hidden,
        2 * (4 * share * depth + depth * hidden + 4 * count * hidden),
        scratch=[pltpu.VMEM((4 * count, depth), bf16), pltpu.VMEM((4, count, TILE), bf16)],
        cost=SHORT,
    )(table, rows, weights)


def head_last_body(table, own, one, two, three, pre, out):
    total = own[...].astype(f32) + one[...].astype(f32)
    total += two[...].astype(f32) + three[...].astype(f32)
    out[...] = (total * unit_slope(pre[: own.shape[0]].astype(f32))).astype(bf16)


def head_last(own, arrived, preact, table):
    count, hidden = own.shape
    share = preact.shape[0] // 4
    width = hidden // 2
    block = pl.BlockSpec((count, width), lambda t, p: (0, t))
    return call(
        head_last_body,
        "head_last",
        (2,),
        1,
        [block] * 4
        + [pl.BlockSpec((share, width), lambda t, p: (p[GZ], t))],
        block,
        jax.ShapeDtypeStruct((count, hidden), bf16),
        count * hidden * 40,
        12 * count * hidden,
        cost=LONG,
    )(table, own, *arrived, preact)


def ready_body(table, own, side_a, side_b, pre, held, partial, slope):
    head = held.shape[0]
    slope[...] = unit_slope(pre[head:].astype(f32)).astype(bf16)
    total = own[...].astype(f32)
    first = pl.program_id(0) < pl.num_programs(0) // 2
    partial[:head] = held[...]

    @pl.when(first)
    def _():
        partial[head:] = (total + side_a[...].astype(f32)).astype(bf16)

    @pl.when(jnp.logical_not(first))
    def _():
        partial[head:] = (total + side_b[...].astype(f32)).astype(bf16)


def halves(count, hidden):
    tiles = hidden // TILE
    return [
        pl.BlockSpec((count, TILE), lambda t, p: (0, jnp.minimum(t, tiles // 2 - 1))),
        pl.BlockSpec((count, TILE), lambda t, p: (0, jnp.maximum(t - tiles // 2, 0))),
    ]


def tail_ready(own, side_a, side_b, preact, table, held):
    count, hidden = own.shape
    share = preact.shape[0] // 4
    block = pl.BlockSpec((count, TILE), lambda t, p: (0, t))
    return call(
        ready_body,
        "tail_ready",
        (hidden // TILE,),
        1,
        [block]
        + halves(count, hidden)
        + [
            pl.BlockSpec((share, TILE), lambda t, p: (p[GZ], t)),
            pl.BlockSpec((share - count, TILE), lambda t, p: (0, t)),
        ],
        [pl.BlockSpec((share, TILE), lambda t, p: (0, t)), block],
        [jax.ShapeDtypeStruct((share, hidden), bf16), jax.ShapeDtypeStruct((count, hidden), bf16)],
        count * hidden * 40,
        10 * count * hidden,
        cost=SHORT,
    )(table, own, side_a, side_b, preact, held)


def tail_last_body(table, partial, slope, sum_a, sum_b, keep, taken, out, down):
    width = sum_a.shape[1]
    down[...] = (keep[...] + taken[...].astype(f32)).astype(bf16)
    for start, arrived in ((0, sum_a), (width, sum_b)):
        cols = slice(start, start + width)
        total = partial[:, cols].astype(f32) + arrived[...].astype(f32)
        out[:, cols] = (total * slope[:, cols].astype(f32)).astype(bf16)


def tail_last(partial, slope, sum_a, sum_b, keep, taken, table):
    count, hidden = slope.shape
    share = partial.shape[0]
    chunk, features = keep.shape
    step = 32
    start, last = (share - count) // step, count // step - 1
    half = pl.BlockSpec((step, hidden // 2), lambda t, p: (jnp.minimum(t, last), 0))
    whole = pl.BlockSpec((step, hidden), lambda t, p: (start + jnp.minimum(t, last), 0))
    down = pl.BlockSpec((step, features), lambda t, p: (t, 0))
    return call(
        tail_last_body,
        "tail_last",
        (chunk // step,),
        1,
        [
            whole,
            pl.BlockSpec((step, hidden), lambda t, p: (jnp.minimum(t, last), 0)),
            half,
            half,
            down,
            down,
        ],
        [whole, down],
        [
            jax.ShapeDtypeStruct((share, hidden), bf16),
            jax.ShapeDtypeStruct((chunk, features), bf16),
        ],
        count * hidden * 4,
        10 * count * hidden,
        aliases={1: 0},
    )(table, partial, slope, sum_a, sum_b, keep, taken)


def near_body(table, pre_own, pre_partner, own, partner, out):
    total = cols_dot(gelu(pre_own[...].astype(f32)).astype(bf16), own[...])
    total += cols_dot(gelu(pre_partner[...].astype(f32)).astype(bf16), partner[...])
    out[0] = total.astype(bf16)


def near_terms(preact, own, partner, table, at, cost=SHORT):
    rows, hidden = preact.shape
    share, features = own.shape
    chunk = hidden // 8
    return call(
        near_body,
        "near_terms",
        (2,),
        1,
        [
            pl.BlockSpec((share, chunk), lambda t, p: (p[ORDER], p[at + t])),
            pl.BlockSpec((share, chunk), lambda t, p: (p[ORDER + 1], p[at + t])),
            pl.BlockSpec((share, features), lambda t, p: (0, 0)),
            pl.BlockSpec((share, features), lambda t, p: (0, 0)),
        ],
        pl.BlockSpec((1, chunk, features), lambda t, p: (t, 0, 0)),
        jax.ShapeDtypeStruct((2, chunk, features), bf16),
        8 * share * features * chunk,
        2 * (4 * share * chunk + 2 * share * features + 2 * features * chunk),
        cost=cost,
    )(table, preact, preact, own, partner)


def terms_body(near, table, *refs):
    extra = refs[-4] if near else None
    rows, out_a, out_b = refs[-3:]
    total = None
    share = refs[0].shape[0]
    for j, pre in enumerate(refs[: 2 if near else 4]):
        act = gelu(pre[...].astype(f32)).astype(bf16)
        term = cols_dot(act, rows[j])
        total = term if total is None else total + term
    if near:
        total += extra[0].astype(f32)

    @pl.when(pl.program_id(0) == 0)
    def _():
        out_a[...] = total.astype(bf16)

    @pl.when(pl.program_id(0) == 1)
    def _():
        out_b[...] = total.astype(bf16)


def terms(preact, rows, table, at, held=None, cost=SHORT):
    hidden = preact.shape[1]
    _, share, features = rows.shape
    chunk = hidden // 8
    near = held is not None
    pieces = (2, 3) if near else (0, 1, 2, 3)

    def source(j):
        return pl.BlockSpec((share, chunk), lambda t, p: (p[ORDER + j], p[at + t]))

    out = pl.BlockSpec((chunk, features), lambda t, p: (0, 0))
    return call(
        functools.partial(terms_body, near),
        "terms",
        (2,),
        1,
        [source(j) for j in pieces]
        + [pl.BlockSpec((1, chunk, features), lambda t, p: (t, 0, 0))] * near
        + [pl.BlockSpec((len(pieces), share, features), lambda t, p: (int(near), 0, 0))],
        [out, out],
        [jax.ShapeDtypeStruct((chunk, features), bf16)] * 2,
        4 * len(pieces) * share * features * chunk,
        2 * (2 * len(pieces) * share * chunk + len(pieces) * share * features),
        cost=cost,
    )(table, *[preact] * len(pieces), *([held] if near else []), rows)


def shards(preact, grad_output, down_weight):
    gy = lax.axis_index("gy")
    gz = lax.axis_index("gz")
    gx = lax.axis_index("gx")
    y, h = gx % 4, gx // 4
    entries = [gy ^ j for j in range(4)]
    entries += [(gz + 2) % 4 ^ gy, (gz + 1) % 4 ^ gy, (gz + 3) % 4 ^ gy, gz ^ gy, gz, 0]
    up, down, far = (y + 1) % 4, (y + 3) % 4, (y + 2) % 4
    entries += [far, 4 + far, up, 4 + down, down, 4 + up, y, 4 + y]
    table = jnp.stack([jnp.asarray(entry, jnp.int32) for entry in entries])

    other_chip, other_core = gy_move(1, 0), gy_move(0, 1)
    z_up, z_down, z_far = gz_ring(1), gz_ring(-1), gz_ring(2)
    y_up, y_down = gx_move(0, 1), gx_move(0, -1)

    def add(*values):
        return sum(value.astype(f32) for value in values)

    own_head, own_tail = grad_output[:HEAD], grad_output[HEAD:]
    across = lax.ppermute(own_head, "gy", other_chip)
    partner = lax.ppermute(grad_output, "gy", other_core)
    near_far = near_terms(preact, grad_output, partner, table, C_FAR)
    table = after(table, near_far)
    corner = lax.ppermute(after(across, table), "gy", other_core)
    across_tail = lax.ppermute(after(own_tail, across, table), "gy", other_chip)

    head = jnp.stack((own_head, partner[:HEAD], across, corner))
    to_up, to_down, to_far, own = first_parts(head, down_weight, table)
    table = after(table, own)
    arrived = [
        lax.ppermute(to_up, "gz", z_up),
        lax.ppermute(to_down, "gz", z_down),
        lax.ppermute(to_far, "gz", z_far),
    ]

    across_tail = after(across_tail, table)
    corner_tail = [
        lax.ppermute(across_tail[start : start + PIECE], "gy", other_core)
        for start in range(0, across_tail.shape[0], PIECE)
    ]
    rows = jnp.stack(
        (
            grad_output,
            partner,
            lax.optimization_barrier(jnp.concatenate((across, across_tail))),
            lax.optimization_barrier(jnp.concatenate((corner, *corner_tail))),
        )
    )

    c_far, d_far = terms(preact, rows, table, C_FAR, near_far)
    table = after(table, c_far)
    c_far = lax.ppermute(c_far, "gx", y_down)
    d_far = lax.ppermute(d_far, "gx", y_up)

    a_far, b_far, a_side, b_side, a_sum, b_sum, own_tail = tail_parts(rows, down_weight, table)
    table = after(table, own_tail)
    a_far = lax.ppermute(after(a_far, *arrived), "gz", z_down)
    b_far = lax.ppermute(after(b_far, *arrived), "gz", z_up)
    table = after(table, *arrived)

    c_side, d_side = terms(preact, rows, table, C_SIDE)
    table = after(table, c_side)
    c_side = lax.ppermute(after(c_side, c_far, d_far), "gx", y_up)
    d_side = lax.ppermute(after(d_side, c_far, d_far), "gx", y_down)

    table = after(table, c_far, d_far)
    c_sum, d_sum = terms(preact, rows, table, C_SUM, cost=MID)
    table = after(table, c_sum)
    a_side = lax.ppermute(after(a_side, table, a_far, b_far), "gz", z_up)
    b_side = lax.ppermute(after(b_side, table, a_far, b_far), "gz", z_down)
    a_sum = add(a_sum, after(a_far, table)).astype(bf16)
    b_sum = add(b_sum, after(b_far, table)).astype(bf16)
    c_sum = add(c_sum, c_far).astype(bf16)
    d_sum = add(d_sum, d_far).astype(bf16)
    table = after(table, a_sum, b_sum, c_sum)

    c_sum = lax.ppermute(after(c_sum, c_side, d_side), "gx", y_down)
    d_sum = lax.ppermute(after(d_sum, c_side, d_side), "gx", y_up)
    table = after(table, c_side, d_side)

    c_own, d_own = terms(preact, rows, table, C_OWN, cost=LAST)
    table = after(table, c_own)

    held = head_last(own, arrived, preact, table)
    table = after(table, held)

    a_sum = lax.ppermute(after(a_sum, table, a_side, b_side), "gz", z_down)
    b_sum = lax.ppermute(after(b_sum, table, a_side, b_side), "gz", z_up)

    c_sum, d_sum = after(c_sum, table, a_side, b_side), after(d_sum, table, a_side, b_side)
    c_own = add(c_own, c_side, c_sum)
    d_own = add(d_own, d_side, d_sum)
    keep = jnp.where(h == 0, c_own, d_own)
    give = jnp.where(h == 0, d_own, c_own).astype(bf16)
    taken = lax.ppermute(give, "gx", gx_move(1, 0))
    own_tail = after(own_tail, give)
    partial, slope = tail_ready(own_tail, a_side, b_side, preact, table, held)
    grad_pre, grad_down = tail_last(partial, slope, a_sum, b_sum, keep, taken, table)
    return (grad_pre, grad_down)


def solution(mesh):
    return jax.shard_map(
        shards,
        mesh=mesh,
        in_specs=(P("gx", "gy"), P(("gx", "gy"), "gz"), P("gy", "gz")),
        out_specs=(P(("gx", "gz"), "gy"), P(("gy", "gx"), "gz")),
        check_vma=False,
    )
```

```python
import functools
import math

import jax
import jax.numpy as jnp
from jax import lax
from jax.experimental import pallas as pl
from jax.experimental.pallas import tpu as pltpu
from jax.sharding import PartitionSpec as P

root_half = 1.0 / math.sqrt(2.0)
slope_scale = 1.0 / math.sqrt(2.0 * math.pi)
bf16 = jnp.bfloat16
f32 = jnp.float32
HEAD = 144
TILE = 512
PIECE = 96
SHORT, MID, LAST, LONG = 1 / 64, 2, 1 / 64, 1 / 64
VMEM = 63 * 1024 * 1024


def gelu(values):
    return 0.5 * values * (1.0 + lax.erf(values * root_half))


def unit_slope(values):
    return (
        0.5 * (1.0 + lax.erf(values * root_half))
        + values * jnp.exp(-0.5 * values * values) * slope_scale
    )


def gz_ring(step):
    return [(i, (i + step) % 4) for i in range(4)]


def gx_move(dh, dy):
    return [(h * 4 + y, (h + dh) % 2 * 4 + (y + dy) % 4) for h in range(2) for y in range(4)]


def gy_move(dl, dc):
    return [(l * 2 + c, (l + dl) % 2 * 2 + (c + dc) % 2) for l in range(2) for c in range(2)]


def after(value, *others):
    return lax.optimization_barrier((value,) + others)[0]


def call(body, name, grid, prefetch, in_specs, out_specs, out_shape, flops, moved, scratch=(), cost=1, aliases=None):
    return pl.pallas_call(
        body,
        name=name,
        out_shape=out_shape,
        grid_spec=pltpu.PrefetchScalarGridSpec(
            num_scalar_prefetch=prefetch, grid=grid, in_specs=in_specs, out_specs=out_specs,
            scratch_shapes=list(scratch),
        ),
        compiler_params=pltpu.CompilerParams(
            dimension_semantics=("arbitrary",) * len(grid), vmem_limit_bytes=VMEM
        ),
        input_output_aliases=aliases or {},
        cost_estimate=pl.CostEstimate(
            flops=int(flops * cost), bytes_accessed=int(moved * cost), transcendentals=0
        ),
    )


def rows_dot(rows, weights):
    return lax.dot_general(rows, weights, (((1,), (1,)), ((), ())), preferred_element_type=f32)


def cols_dot(left, right):
    return lax.dot_general(left, right, (((0,), (0,)), ((), ())), preferred_element_type=f32)


ORDER, FAR, UP, DOWN, OWN, GZ = 0, 4, 5, 6, 7, 8
C_FAR, C_SIDE, C_SUM, C_OWN = 10, 12, 14, 16


def first_body(table, rows, weights, up, down, far, own, part):
    count = up.shape[0]
    total = rows_dot(rows[...], weights[...]).astype(bf16)
    for j in range(4):
        part[j] = total[j * count : (j + 1) * count]
    up[...] = part[table[UP]]
    down[...] = part[table[DOWN]]
    far[...] = part[table[FAR]]
    own[...] = part[table[OWN]]


def first_parts(rows, weights, table):
    _, count, depth = rows.shape
    hidden = weights.shape[0]
    block = pl.BlockSpec((count, TILE), lambda t, o: (0, t))
    return call(
        first_body,
        "first_parts",
        (hidden // TILE,),
        1,
        [
            pl.BlockSpec((4 * count, depth), lambda t, o: (0, 0)),
            pl.BlockSpec((TILE, depth), lambda t, o: (t, 0)),
        ],
        [block] * 4,
        [jax.ShapeDtypeStruct((count, hidden), bf16)] * 4,
        8 * count * depth * hidden,
        2 * (4 * count * depth + depth * hidden + 4 * count * hidden),
        scratch=[pltpu.VMEM((4, count, TILE), bf16)],
        cost=SHORT,
    )(table, rows.reshape(4 * count, depth), weights)


def tail_body(table, rows, weights, far_a, far_b, side_a, side_b, sum_a, sum_b, own, left, part):
    count = own.shape[0]
    first = pl.program_id(0) < pl.num_programs(0) // 2

    @pl.when(pl.program_id(0) == 0)
    def _():
        for j in range(4):
            left[j * count : (j + 1) * count] = rows[j, HEAD:]

    total = rows_dot(left[...], weights[...]).astype(bf16)
    for j in range(4):
        part[j] = total[j * count : (j + 1) * count]
    own[...] = part[table[OWN]]

    @pl.when(first)
    def _():
        far_a[...] = part[table[FAR]]
        side_a[...] = part[table[UP]]
        sum_a[...] = part[table[DOWN]]

    @pl.when(jnp.logical_not(first))
    def _():
        far_b[...] = part[table[FAR]]
        side_b[...] = part[table[DOWN]]
        sum_b[...] = part[table[UP]]


def tail_parts(rows, weights, table):
    _, share, depth = rows.shape
    count = share - HEAD
    hidden = weights.shape[0]
    tiles = hidden // TILE
    half_a = pl.BlockSpec((count, TILE), lambda t, p: (0, jnp.minimum(t, tiles // 2 - 1)))
    half_b = pl.BlockSpec((count, TILE), lambda t, p: (0, jnp.maximum(t - tiles // 2, 0)))
    half = jax.ShapeDtypeStruct((count, hidden // 2), bf16)
    return call(
        tail_body,
        "tail_parts",
        (tiles,),
        1,
        [
            pl.BlockSpec((4, share, depth), lambda t, o: (0, 0, 0)),
            pl.BlockSpec((TILE, depth), lambda t, o: (t, 0)),
        ],
        [half_a, half_b] * 3 + [pl.BlockSpec((count, TILE), lambda t, o: (0, t))],
        [half] * 6 + [jax.ShapeDtypeStruct((count, hidden), bf16)],
        8 * count * depth * hidden,
        2 * (4 * share * depth + depth * hidden + 4 * count * hidden),
        scratch=[pltpu.VMEM((4 * count, depth), bf16), pltpu.VMEM((4, count, TILE), bf16)],
        cost=SHORT,
    )(table, rows, weights)


def head_last_body(table, own, one, two, three, pre, out):
    total = own[...].astype(f32) + one[...].astype(f32)
    total += two[...].astype(f32) + three[...].astype(f32)
    out[...] = (total * unit_slope(pre[: own.shape[0]].astype(f32))).astype(bf16)


def head_last(own, arrived, preact, table):
    count, hidden = own.shape
    share = preact.shape[0] // 4
    width = hidden // 2
    block = pl.BlockSpec((count, width), lambda t, p: (0, t))
    return call(
        head_last_body,
        "head_last",
        (2,),
        1,
        [block] * 4
        + [pl.BlockSpec((share, width), lambda t, p: (p[GZ], t))],
        block,
        jax.ShapeDtypeStruct((count, hidden), bf16),
        count * hidden * 40,
        12 * count * hidden,
        cost=LONG,
    )(table, own, *arrived, preact)


def ready_body(table, own, side_a, side_b, pre, held, partial, slope):
    head = held.shape[0]
    slope[...] = unit_slope(pre[head:].astype(f32)).astype(bf16)
    total = own[...].astype(f32)
    first = pl.program_id(0) < pl.num_programs(0) // 2
    partial[:head] = held[...]

    @pl.when(first)
    def _():
        partial[head:] = (total + side_a[...].astype(f32)).astype(bf16)

    @pl.when(jnp.logical_not(first))
    def _():
        partial[head:] = (total + side_b[...].astype(f32)).astype(bf16)


def halves(count, hidden):
    tiles = hidden // TILE
    return [
        pl.BlockSpec((count, TILE), lambda t, p: (0, jnp.minimum(t, tiles // 2 - 1))),
        pl.BlockSpec((count, TILE), lambda t, p: (0, jnp.maximum(t - tiles // 2, 0))),
    ]


def tail_ready(own, side_a, side_b, preact, table, held):
    count, hidden = own.shape
    share = preact.shape[0] // 4
    block = pl.BlockSpec((count, TILE), lambda t, p: (0, t))
    return call(
        ready_body,
        "tail_ready",
        (hidden // TILE,),
        1,
        [block]
        + halves(count, hidden)
        + [
            pl.BlockSpec((share, TILE), lambda t, p: (p[GZ], t)),
            pl.BlockSpec((share - count, TILE), lambda t, p: (0, t)),
        ],
        [pl.BlockSpec((share, TILE), lambda t, p: (0, t)), block],
        [jax.ShapeDtypeStruct((share, hidden), bf16), jax.ShapeDtypeStruct((count, hidden), bf16)],
        count * hidden * 40,
        10 * count * hidden,
        cost=SHORT,
    )(table, own, side_a, side_b, preact, held)


def tail_last_body(table, partial, slope, sum_a, sum_b, keep, taken, out, down):
    head = out.shape[0] - slope.shape[0]
    out[:head] = partial[:head]
    down[...] = (keep[...].astype(f32) + taken[...].astype(f32)).astype(bf16)
    total = partial[head:].astype(f32)
    first = pl.program_id(0) < pl.num_programs(0) // 2

    @pl.when(first)
    def _():
        out[head:] = ((total + sum_a[...].astype(f32)) * slope[...].astype(f32)).astype(bf16)

    @pl.when(jnp.logical_not(first))
    def _():
        out[head:] = ((total + sum_b[...].astype(f32)) * slope[...].astype(f32)).astype(bf16)


def tail_last(partial, slope, sum_a, sum_b, keep, taken, table):
    count, hidden = slope.shape
    share = partial.shape[0]
    chunk, features = keep.shape
    tiles = hidden // TILE
    whole = pl.BlockSpec((share, TILE), lambda t, p: (0, t))
    down = pl.BlockSpec((chunk // tiles, features), lambda t, p: (t, 0))
    return call(
        tail_last_body,
        "tail_last",
        (tiles,),
        1,
        [whole, pl.BlockSpec((count, TILE), lambda t, p: (0, t))]
        + halves(count, hidden)
        + [down, down],
        [whole, down],
        [
            jax.ShapeDtypeStruct((share, hidden), bf16),
            jax.ShapeDtypeStruct((chunk, features), bf16),
        ],
        count * hidden * 4,
        10 * count * hidden,
    )(table, partial, slope, sum_a, sum_b, keep, taken)


def near_body(table, pre_own, pre_partner, own, partner, out):
    total = cols_dot(gelu(pre_own[...].astype(f32)).astype(bf16), own[...])
    total += cols_dot(gelu(pre_partner[...].astype(f32)).astype(bf16), partner[...])
    out[0] = total.astype(bf16)


def near_terms(preact, own, partner, table, at, cost=SHORT):
    rows, hidden = preact.shape
    share, features = own.shape
    chunk = hidden // 8
    return call(
        near_body,
        "near_terms",
        (2,),
        1,
        [
            pl.BlockSpec((share, chunk), lambda t, p: (p[ORDER], p[at + t])),
            pl.BlockSpec((share, chunk), lambda t, p: (p[ORDER + 1], p[at + t])),
            pl.BlockSpec((share, features), lambda t, p: (0, 0)),
            pl.BlockSpec((share, features), lambda t, p: (0, 0)),
        ],
        pl.BlockSpec((1, chunk, features), lambda t, p: (t, 0, 0)),
        jax.ShapeDtypeStruct((2, chunk, features), bf16),
        8 * share * features * chunk,
        2 * (4 * share * chunk + 2 * share * features + 2 * features * chunk),
        cost=cost,
    )(table, preact, preact, own, partner)


def terms_body(near, table, *refs):
    extra = refs[-4] if near else None
    rows, out_a, out_b = refs[-3:]
    total = None
    share = refs[0].shape[0]
    for j, pre in enumerate(refs[: 2 if near else 4]):
        act = gelu(pre[...].astype(f32)).astype(bf16)
        term = cols_dot(act, rows[j])
        total = term if total is None else total + term
    if near:
        total += extra[0].astype(f32)

    @pl.when(pl.program_id(0) == 0)
    def _():
        out_a[...] = total.astype(bf16)

    @pl.when(pl.program_id(0) == 1)
    def _():
        out_b[...] = total.astype(bf16)


def terms(preact, rows, table, at, held=None, cost=SHORT):
    hidden = preact.shape[1]
    _, share, features = rows.shape
    chunk = hidden // 8
    near = held is not None
    pieces = (2, 3) if near else (0, 1, 2, 3)

    def source(j):
        return pl.BlockSpec((share, chunk), lambda t, p: (p[ORDER + j], p[at + t]))

    out = pl.BlockSpec((chunk, features), lambda t, p: (0, 0))
    return call(
        functools.partial(terms_body, near),
        "terms",
        (2,),
        1,
        [source(j) for j in pieces]
        + [pl.BlockSpec((1, chunk, features), lambda t, p: (t, 0, 0))] * near
        + [pl.BlockSpec((len(pieces), share, features), lambda t, p: (int(near), 0, 0))],
        [out, out],
        [jax.ShapeDtypeStruct((chunk, features), bf16)] * 2,
        4 * len(pieces) * share * features * chunk,
        2 * (2 * len(pieces) * share * chunk + len(pieces) * share * features),
        cost=cost,
    )(table, *[preact] * len(pieces), *([held] if near else []), rows)


def shards(preact, grad_output, down_weight):
    gy = lax.axis_index("gy")
    gz = lax.axis_index("gz")
    gx = lax.axis_index("gx")
    y, h = gx % 4, gx // 4
    entries = [gy ^ j for j in range(4)]
    entries += [(gz + 2) % 4 ^ gy, (gz + 1) % 4 ^ gy, (gz + 3) % 4 ^ gy, gz ^ gy, gz, 0]
    up, down, far = (y + 1) % 4, (y + 3) % 4, (y + 2) % 4
    entries += [far, 4 + far, up, 4 + down, down, 4 + up, y, 4 + y]
    table = jnp.stack([jnp.asarray(entry, jnp.int32) for entry in entries])

    other_chip, other_core = gy_move(1, 0), gy_move(0, 1)
    z_up, z_down, z_far = gz_ring(1), gz_ring(-1), gz_ring(2)
    y_up, y_down = gx_move(0, 1), gx_move(0, -1)

    def add(*values):
        return sum(value.astype(f32) for value in values)

    own_head, own_tail = grad_output[:HEAD], grad_output[HEAD:]
    across = lax.ppermute(own_head, "gy", other_chip)
    partner = lax.ppermute(grad_output, "gy", other_core)
    near_far = near_terms(preact, grad_output, partner, table, C_FAR)
    table = after(table, near_far)
    corner = lax.ppermute(after(across, table), "gy", other_core)
    across_tail = lax.ppermute(after(own_tail, across, table), "gy", other_chip)

    head = jnp.stack((own_head, partner[:HEAD], across, corner))
    to_up, to_down, to_far, own = first_parts(head, down_weight, table)
    table = after(table, own)
    arrived = [
        lax.ppermute(to_up, "gz", z_up),
        lax.ppermute(to_down, "gz", z_down),
        lax.ppermute(to_far, "gz", z_far),
    ]

    across_tail = after(across_tail, table)
    corner_tail = [
        lax.ppermute(across_tail[start : start + PIECE], "gy", other_core)
        for start in range(0, across_tail.shape[0], PIECE)
    ]
    rows = jnp.stack(
        (
            grad_output,
            partner,
            lax.optimization_barrier(jnp.concatenate((across, across_tail))),
            lax.optimization_barrier(jnp.concatenate((corner, *corner_tail))),
        )
    )

    c_far, d_far = terms(preact, rows, table, C_FAR, near_far)
    table = after(table, c_far)
    c_far = lax.ppermute(c_far, "gx", y_down)
    d_far = lax.ppermute(d_far, "gx", y_up)

    a_far, b_far, a_side, b_side, a_sum, b_sum, own_tail = tail_parts(rows, down_weight, table)
    table = after(table, own_tail)
    a_far = lax.ppermute(after(a_far, *arrived), "gz", z_down)
    b_far = lax.ppermute(after(b_far, *arrived), "gz", z_up)
    table = after(table, *arrived)

    c_side, d_side = terms(preact, rows, table, C_SIDE)
    table = after(table, c_side)
    c_side = lax.ppermute(after(c_side, c_far, d_far), "gx", y_up)
    d_side = lax.ppermute(after(d_side, c_far, d_far), "gx", y_down)

    table = after(table, c_far, d_far)
    c_sum, d_sum = terms(preact, rows, table, C_SUM, cost=MID)
    table = after(table, c_sum)
    a_side = lax.ppermute(after(a_side, table, a_far, b_far), "gz", z_up)
    b_side = lax.ppermute(after(b_side, table, a_far, b_far), "gz", z_down)
    a_sum = add(a_sum, after(a_far, table)).astype(bf16)
    b_sum = add(b_sum, after(b_far, table)).astype(bf16)
    c_sum = add(c_sum, c_far).astype(bf16)
    d_sum = add(d_sum, d_far).astype(bf16)
    table = after(table, a_sum, b_sum, c_sum)

    c_sum = lax.ppermute(after(c_sum, c_side, d_side), "gx", y_down)
    d_sum = lax.ppermute(after(d_sum, c_side, d_side), "gx", y_up)
    table = after(table, c_side, d_side)

    c_own, d_own = terms(preact, rows, table, C_OWN, cost=LAST)
    table = after(table, c_own)

    held = head_last(own, arrived, preact, table)
    table = after(table, held)

    a_sum = lax.ppermute(after(a_sum, table, a_side, b_side), "gz", z_down)
    b_sum = lax.ppermute(after(b_sum, table, a_side, b_side), "gz", z_up)

    c_sum, d_sum = after(c_sum, table, a_side, b_side), after(d_sum, table, a_side, b_side)
    c_own = add(c_own, c_side, c_sum)
    d_own = add(d_own, d_side, d_sum)
    keep = jnp.where(h == 0, c_own, d_own).astype(bf16)
    give = jnp.where(h == 0, d_own, c_own).astype(bf16)
    taken = lax.ppermute(give, "gx", gx_move(1, 0))
    own_tail = after(own_tail, give)
    partial, slope = tail_ready(own_tail, a_side, b_side, preact, table, held)
    grad_pre, grad_down = tail_last(partial, slope, a_sum, b_sum, keep, taken, table)
    return (grad_pre, grad_down)


def solution(mesh):
    return jax.shard_map(
        shards,
        mesh=mesh,
        in_specs=(P("gx", "gy"), P(("gx", "gy"), "gz"), P("gy", "gz")),
        out_specs=(P(("gx", "gz"), "gy"), P(("gy", "gx"), "gz")),
        check_vma=False,
    )
```
